512 devices in a mesh: group: 16 (over z), shard: 32 (over y, x, core).
Axes of the slice: x: 4, y: 4, z: 16, core: 2. Of those that a mesh axis runs over, the one named last changes fastest.
Arguments:
- hot_row: int32 [4096, 39], P(('group', 'shard')), may hold values from 0 to 2047
- cold_row: int32 [4096, 39], P(('group', 'shard')), may hold values from 0 to 4095
- cold_owner: int32 [4096, 39], P(('group', 'shard')), may hold values from 0 to 31, as said below
- is_cold: int32 [4096, 39], P(('group', 'shard')), may hold values from 0 to 1
- grad_logit: float32 [4096], P(('group', 'shard')), may hold values from -12 to 12
- hot_table: bfloat16 [2048, 128], replicated, may hold values from -6 to 6
- cold_table: bfloat16 [131072, 128], P('shard'), may hold values from -6 to 6
- first_weight: bfloat16 [100, 1521], replicated, may hold values from -0.15625 to 0.15625
- second_weight: bfloat16 [100, 3900], replicated, may hold values from -0.09375 to 0.09375
- third_weight: bfloat16 [100, 3900], replicated, may hold values from -0.09375 to 0.09375
- out_weight: float32 [3, 100], replicated, may hold values from -0.375 to 0.375
Outputs:
- hot_grad: bfloat16 [2048, 128], replicated
- cold_grad: bfloat16 [131072, 128], P('shard')
- logits: float32 [4096], P(('group', 'shard'))
The draws below stay inside these ranges and needn't reach their ends.
Inputs may be any that keep to these rules, and one draw needn't show every extreme that they name: `cold_owner`: among the 312 lookups of one device, at most 9 with is_cold 1 name the same owner; for each index of group, one owner receives exactly 9 such lookups from every device of that group index.
All inputs are finite; a program needn't handle non-finite values.
Results may differ from the reference program's by a relative error of at most 0.014.
Values may be sent and summed in bfloat16 or wider, within the bound.
No kernel may reach another device: no remote copies, remote signals or barrier semaphores. Data moves between devices by JAX's collectives and lax.ppermute only.
A program may use at most 64 MiB of HBM per device.

```python
import jax
import jax.numpy as jnp
from jax import lax

E = 128
F = 39
H = 100
B_DEV = 8
HOT_ROWS = 2048
CR_DEV = 4096
SAMPLES = 4096
COLD_ROWS = 131072
CAP = 9
N_SHARD = 32


def plan_lookups(key):
    blocks = SAMPLES // B_DEV
    lookups = B_DEV * F
    groups = blocks // N_SHARD
    heavy = jax.random.randint(jax.random.fold_in(key, 11), (groups,), 0, N_SHARD)
    counts = jax.random.randint(jax.random.fold_in(key, 12), (blocks, N_SHARD), 0, CAP + 1)
    block_group = jnp.arange(blocks, dtype=jnp.int32) // N_SHARD
    forced = heavy[block_group][:, None] == jnp.arange(N_SHARD, dtype=jnp.int32)[None, :]
    counts = jnp.where(forced, CAP, counts)
    ends = jnp.cumsum(counts, axis=1)
    totals = ends[:, -1:]
    position = jnp.arange(lookups, dtype=jnp.int32)
    sorted_owner = jnp.sum((ends[:, None, :] <= position[None, :, None]).astype(jnp.int32), axis=2)
    sorted_cold = (position[None, :] < totals).astype(jnp.int32)
    filler = jax.random.randint(jax.random.fold_in(key, 13), (blocks, lookups), 0, N_SHARD)
    sorted_owner = jnp.where(sorted_cold == 1, sorted_owner, filler)
    block_keys = jax.random.split(jax.random.fold_in(key, 14), blocks)
    orders = jax.vmap(lambda block_key: jax.random.permutation(block_key, lookups))(block_keys)
    owner = jnp.take_along_axis(sorted_owner, orders, axis=1)
    coldness = jnp.take_along_axis(sorted_cold, orders, axis=1)
    return (owner.reshape(SAMPLES, F).astype(jnp.int32), coldness.reshape(SAMPLES, F).astype(jnp.int32))


def draw_cold_owner(key, part):
    return plan_lookups(key)[0]


def draw_is_cold(key, part):
    return plan_lookups(key)[1]


def draw_hot_row(key, part):
    blocks = SAMPLES // B_DEV
    upper = jax.random.randint(jax.random.fold_in(key, 21), (SAMPLES, F), 1, HOT_ROWS + 1)
    ranked = jax.random.randint(jax.random.fold_in(key, 22), (SAMPLES, F), 0, upper)
    order = jax.random.permutation(jax.random.fold_in(key, 23), HOT_ROWS).astype(jnp.int32)
    common = order[ranked]
    block_index = jnp.arange(SAMPLES, dtype=jnp.int32) // B_DEV
    start = block_index * HOT_ROWS // blocks
    reach = max(1, HOT_ROWS // blocks)
    offset = jax.random.randint(jax.random.fold_in(key, 24), (SAMPLES, F), 0, reach)
    local = (start[:, None] + offset) % HOT_ROWS
    choose = jax.random.randint(jax.random.fold_in(key, 25), (SAMPLES, F), 0, 2)
    return jnp.where(choose == 1, local, common).astype(jnp.int32)


def touch_ends(array, rng, low, largest):
    longest = array.shape.index(max(array.shape))
    spots = []
    for shift in (0, 1):
        where = [jax.random.randint(jax.random.fold_in(rng, axis), (), 0, length) for axis, length in enumerate(array.shape)]
        where[longest] = (where[longest] + shift) % array.shape[longest]
        spots.append(tuple(where))
    return array.at[spots[0]].set(low).at[spots[1]].set(largest)


def level_of(stream_key, shape, cuts, smallest, top_value):
    def one(dim, blocks):
        draws = jax.random.uniform(jax.random.fold_in(jax.random.fold_in(stream_key, 6), dim), (blocks,), jnp.float32, smallest / len(cuts), top_value / len(cuts))
        return jnp.repeat(jnp.exp(draws), shape[dim] // blocks).reshape((-1,) + (1,) * (len(shape) - dim - 1))

    level = one(*cuts[0])
    for cut in cuts[1:]:
        level = level * one(*cut)
    return level


def centred(rng, extent, width, most, shards=(), held_as=jnp.bfloat16):
    drawn = jax.random.normal(rng, extent, jnp.float32) * width
    if len(shards) > 0:
        drawn = level_of(rng, extent, shards, -0.22, 0.18) * drawn
    return jnp.clip(drawn, min=-most, max=most).astype(held_as)


def setup_inputs(seed: int = 0) -> dict:
    keys = jax.random.split(jax.random.key(seed), 12)
    hot_row = draw_hot_row(jax.random.fold_in(keys[11], 71), 0)
    cold_row = touch_ends(jax.random.randint(keys[1], (SAMPLES, F), 0, CR_DEV), jax.random.fold_in(keys[1], 1), 0, CR_DEV - 1).astype(jnp.int32)
    cold_owner = draw_cold_owner(jax.random.fold_in(keys[11], 71), 0)
    is_cold = draw_is_cold(jax.random.fold_in(keys[11], 71), 0)
    grad_logit = centred(keys[4], (SAMPLES,), 2.0, 12.0, ((0, 512),), jnp.float32)
    hot_table = centred(keys[5], (HOT_ROWS, E), 1.0, 6.0)
    cold_table = centred(keys[6], (COLD_ROWS, E), 1.0, 6.0, ((0, 32),))
    first_weight = centred(keys[7], (H, F * F), (F * F) ** -0.5, 0.15625)
    second_weight = centred(keys[8], (H, H * F), (H * F) ** -0.5, 0.09375)
    third_weight = centred(keys[9], (H, H * F), (H * F) ** -0.5, 0.09375)
    out_weight = centred(keys[10], (3, H), (3 * H) ** -0.5, 0.375, (), jnp.float32)
    return dict(hot_row=hot_row, cold_row=cold_row, cold_owner=cold_owner, is_cold=is_cold, grad_logit=grad_logit, hot_table=hot_table, cold_table=cold_table, first_weight=first_weight, second_weight=second_weight, third_weight=third_weight, out_weight=out_weight)


def block_pass(embedded, grad_logit, layer_weights, out_weight):
    batch_rows, fields, breadth = embedded.shape
    base_wide = embedded.astype(jnp.float32)
    previous = embedded
    layer_inputs = []
    logit_sum = jnp.zeros((batch_rows,), jnp.float32)
    for section_index in range(len(layer_weights)):
        weight = layer_weights[section_index]
        below_maps = previous.shape[1]
        outer_rows = (previous.astype(jnp.float32)[:, :, None, :] * base_wide[:, None, :, :]).astype(jnp.bfloat16)
        outer_rows = outer_rows.reshape(batch_rows, below_maps * fields, breadth)
        current = jnp.einsum("hk,bke->bhe", weight.astype(jnp.float32), outer_rows.astype(jnp.float32)).astype(jnp.bfloat16)
        pooled = jnp.sum(current.astype(jnp.float32), axis=2)
        logit_sum = logit_sum + jnp.sum(pooled * out_weight[section_index][None, :], axis=1)
        layer_inputs.append(previous)
        previous = current
    grad_embedded = jnp.zeros((batch_rows, fields, breadth), jnp.float32)
    carried = jnp.zeros((batch_rows, out_weight.shape[1], breadth), jnp.float32)
    for section_index in reversed(range(len(layer_weights))):
        weight = layer_weights[section_index]
        lower_state = layer_inputs[section_index]
        below_maps = lower_state.shape[1]
        grad_state = carried + grad_logit[:, None, None] * out_weight[section_index][None, :, None]
        grad_low = grad_state.astype(jnp.bfloat16)
        grad_outer = jnp.einsum("hk,bhe->bke", weight.astype(jnp.float32), grad_low.astype(jnp.float32))
        grad_outer = grad_outer.reshape(batch_rows, below_maps, fields, breadth)
        grad_embedded = grad_embedded + jnp.sum(grad_outer * lower_state.astype(jnp.float32)[:, :, None, :], axis=1)
        carried = jnp.sum(grad_outer * base_wide[:, None, :, :], axis=2)
    grad_embedded = grad_embedded + carried
    return logit_sum, grad_embedded


def reference(hot_row, cold_row, cold_owner, is_cold, grad_logit, hot_table, cold_table, first_weight, second_weight, third_weight, out_weight):
    layer_weights = (first_weight, second_weight, third_weight)
    global_cold = (cold_owner * CR_DEV + cold_row).astype(jnp.int32)
    cold_flag = is_cold == 1
    embedded = jnp.where(cold_flag[:, :, None], jnp.take(cold_table, global_cold, axis=0), jnp.take(hot_table, hot_row, axis=0))
    blocks = SAMPLES // B_DEV
    embedded_blocks = embedded.reshape(blocks, B_DEV, F, E)
    grad_blocks = grad_logit.reshape(blocks, B_DEV)

    def one_block(block_pair):
        return block_pass(block_pair[0], block_pair[1], layer_weights, out_weight)

    logit_blocks, gradients = lax.map(one_block, (embedded_blocks, grad_blocks))
    gradients = gradients.reshape(SAMPLES * F, E)
    flag_flat = cold_flag.reshape(SAMPLES * F)
    hot_terms = jnp.where(flag_flat[:, None], 0.0, gradients)
    cold_terms = jnp.where(flag_flat[:, None], gradients, 0.0)
    hot_sum = jax.ops.segment_sum(hot_terms, hot_row.reshape(SAMPLES * F), num_segments=HOT_ROWS)
    cold_sum = jax.ops.segment_sum(cold_terms, global_cold.reshape(SAMPLES * F), num_segments=COLD_ROWS)
    return hot_sum.astype(jnp.bfloat16), cold_sum.astype(jnp.bfloat16), logit_blocks.reshape(SAMPLES)
```

```python
import functools

import jax
import jax.numpy as jnp
from jax import lax
from jax.experimental import pallas as pl
from jax.experimental.pallas import tpu as pltpu
from jax.sharding import PartitionSpec as P

CAP = 9
SLOT = 16
FP = 40
VMEM = pl.BlockSpec(memory_space=pltpu.VMEM)
SMEM = pl.BlockSpec(memory_space=pltpu.SMEM)
F32 = jnp.float32
BF16 = jnp.bfloat16
I32 = jnp.int32


def iota(shape, dim):
    return lax.broadcasted_iota(I32, shape, dim)


def route_kernel(owners, hot_ref, row_ref, owner_ref, cold_ref, ask_ref, slot_ref, want_ref, pad_ref):
    samples, fields = hot_ref.shape
    total = samples * FP
    code = jnp.where(cold_ref[...] == 1, owner_ref[...], -1)
    pad_ref[...] = jnp.full(pad_ref.shape, -1.0, F32)
    pad_ref[0:samples, 0:fields] = code.astype(F32)
    pad_ref[samples : 2 * samples, 0:fields] = row_ref[...].astype(F32)
    pad_ref[2 * samples : 3 * samples, 0:fields] = jnp.where(
        cold_ref[...] == 1, -1, hot_ref[...]
    ).astype(F32)
    turned = pad_ref[...].T
    lane = iota((FP, 128), 1).astype(F32)
    for s in range(samples):
        want_ref[s * FP : (s + 1) * FP, :] = jnp.where(
            turned[0:FP, s : s + 1] == lane, 1.0, 0.0
        )
    wanted = want_ref[...]
    below = (iota((total, total), 0) > iota((total, total), 1)).astype(F32).astype(BF16)
    earlier = jnp.dot(below, wanted.astype(BF16), preferred_element_type=F32)
    position = jnp.sum(earlier * wanted, axis=1, keepdims=True)
    lane_all = iota((total, 128), 1).astype(F32)
    owner_col = jnp.sum(wanted * lane_all, axis=1, keepdims=True)
    is_cold = jnp.sum(wanted, axis=1, keepdims=True)
    slot = jnp.where(is_cold > 0.0, owner_col * SLOT + position, -1.0)
    slot_ref[...] = jnp.broadcast_to(slot, (total, 128)).astype(I32)
    row_col = jnp.concatenate(
        [turned[0:FP, samples + s : samples + s + 1] for s in range(samples)], axis=0
    ).astype(I32)
    at = jnp.broadcast_to(position, (total, 128)) == lane_all
    high = jnp.where(at, (row_col >> 6).astype(F32), 0.0).astype(BF16)
    low = jnp.where(at, (row_col & 63).astype(F32), 0.0).astype(BF16)
    there = jnp.where(at, 1.0, 0.0).astype(BF16)
    turned_want = wanted.T[0:owners, :].astype(BF16)
    asked = jnp.dot(
        turned_want, jnp.concatenate([high, low, there], axis=1), preferred_element_type=F32
    )
    row = asked[:, 0:128] * 64.0 + asked[:, 128:256]
    ask_ref[...] = jnp.where(asked[:, 256:384] > 0.0, row, 0.0).astype(I32)


def cin_kernel(
    gl_ref,
    hot_ref,
    cold_ref,
    slot_ref,
    back_ref,
    table_ref,
    out_weight_ref,
    f1_ref,
    f2_ref,
    f3_ref,
    b1_ref,
    b2_ref,
    b3_ref,
    logit_ref,
    outgoing_ref,
    pad_ref,
    pick_ref,
    emb_ref,
    embb_ref,
    x2_ref,
    x3_ref,
    x4_ref,
    outer_ref,
    carry_ref,
    part_ref,
    pool_ref,
    grad_ref,
):
    samples, fields = hot_ref.shape
    total = samples * FP
    breadth = table_ref.shape[1]
    lanes = samples * breadth
    hot_rows = table_ref.shape[0]
    slots = back_ref.shape[0]
    pad_ref[...] = jnp.full(pad_ref.shape, -1.0, F32)
    pad_ref[0:samples, 0:fields] = jnp.where(cold_ref[...] == 1, -1, hot_ref[...]).astype(F32)
    turned = pad_ref[...].T.astype(I32)
    slot = slot_ref[...]

    for s in range(samples):
        ids = turned[0:FP, s : s + 1]
        pick_ref[s * FP : (s + 1) * FP, 0:hot_rows] = (
            jnp.where(ids == iota((FP, hot_rows), 1), 1.0, 0.0).astype(BF16)
        )
    pick_ref[:, hot_rows : hot_rows + slots] = (
        jnp.where(
            jnp.concatenate([slot] * (slots // 128), axis=1) == iota((total, slots), 1), 1.0, 0.0
        ).astype(BF16)
    )
    rows = jnp.dot(pick_ref[:, 0:hot_rows], table_ref[...], preferred_element_type=F32) + jnp.dot(
        pick_ref[:, hot_rows : hot_rows + slots], back_ref[...], preferred_element_type=F32
    )
    emb_ref[...] = jnp.zeros(emb_ref.shape, F32)
    for s in range(samples):
        emb_ref[0:FP, s * breadth : (s + 1) * breadth] = rows[s * FP : (s + 1) * FP, :]
    embb_ref[...] = emb_ref[...].astype(BF16)

    pool_ref[...] = jnp.zeros(pool_ref.shape, F32)
    states = (embb_ref, x2_ref, x3_ref, x4_ref)
    for k, w_ref in enumerate((f1_ref, f2_ref, f3_ref)):
        source = states[k]
        height = source.shape[0]

        def fill(f, _, source=source, height=height):
            line = jnp.broadcast_to(emb_ref[pl.ds(f, 1), :], (16, lanes)).astype(BF16)
            for r in range(0, height, 16):
                at = pl.multiple_of(f * height + r, 16)
                outer_ref[pl.ds(at, 16), :] = source[r : r + 16, :] * line
            return 0

        lax.fori_loop(0, fields, fill, 0)
        depth = fields * height
        weight = w_ref[...]
        for n in range(0, lanes, 256):
            value = jnp.dot(
                weight, outer_ref[0:depth, n : n + 256], preferred_element_type=F32
            ).astype(BF16)
            states[k + 1][:, n : n + 256] = value
            pool_ref[:, n : n + 256] += value.astype(F32) * out_weight_ref[:, k : k + 1]

    for s in range(samples):
        logit_ref[s] = jnp.sum(pool_ref[:, s * breadth : (s + 1) * breadth])

    part_ref[...] = jnp.zeros(part_ref.shape, F32)
    tall = carry_ref.shape[0]
    grad_ref[...] = jnp.zeros(grad_ref.shape, BF16)
    for k, w_ref in reversed(tuple(enumerate((b1_ref, b2_ref, b3_ref)))):
        source = states[k]
        height = source.shape[0]
        for s in range(samples):
            at = slice(s * breadth, (s + 1) * breadth)
            value = jnp.broadcast_to(gl_ref[s] * out_weight_ref[:, k : k + 1], (tall, breadth))
            if k < 2:
                value = value + carry_ref[:, at]
            grad_ref[0:tall, at] = value.astype(BF16)
        carry_ref[0:height, :] = jnp.zeros((height, lanes), F32)

        def back(f, _, source=source, height=height, w_ref=w_ref):
            at = pl.multiple_of(f * height, 16)
            at8 = pl.multiple_of(f * 8, 8)
            for n in range(0, lanes, 256):
                cols = slice(n, n + 256)
                outer = jnp.dot(
                    w_ref[pl.ds(at, height), :], grad_ref[:, cols], preferred_element_type=F32
                )
                carry_ref[0:height, cols] += outer * emb_ref[pl.ds(f, 1), cols]
                mixed = outer * source[:, cols].astype(F32)
                total_rows = mixed[0:8]
                for r in range(8, height, 8):
                    total_rows = total_rows + mixed[r : r + 8]
                part_ref[pl.ds(at8, 8), cols] += total_rows
            return 0

        lax.fori_loop(0, fields, back, 0)

    grads = carry_ref[0:FP, :] + jnp.sum(part_ref[...].reshape(FP, 8, lanes), axis=1)
    stacked = jnp.concatenate(
        [grads[:, s * breadth : (s + 1) * breadth] for s in range(samples)], axis=0
    ).astype(BF16)
    owners = outgoing_ref.shape[0]
    share = hot_rows // owners
    slot_line = slot.astype(F32).T[0:1].astype(I32)
    hot_col = jnp.concatenate([turned[0:FP, s : s + 1] for s in range(samples)], axis=0)
    hot_wide = jnp.broadcast_to(hot_col, (total, 128)).astype(F32).T[0:1].astype(I32)
    line = jnp.where(jnp.broadcast_to(slot_line, (slots, total)) == iota((slots, total), 0), 1.0, 0.0)
    sent_cold = jnp.dot(line.astype(BF16), stacked, preferred_element_type=F32).astype(BF16)
    line = jnp.where(jnp.broadcast_to(hot_wide, (hot_rows, total)) == iota((hot_rows, total), 0), 1.0, 0.0)
    sent_hot = jnp.dot(line.astype(BF16), stacked, preferred_element_type=F32).astype(BF16)
    outgoing_ref[:, 0:SLOT, :] = sent_cold.reshape(owners, SLOT, breadth)
    outgoing_ref[:, SLOT : SLOT + share, :] = sent_hot.reshape(owners, share, breadth)


def call_route(hot_row, cold_row, cold_owner, is_cold, owners):
    samples, fields = hot_row.shape
    total = samples * FP
    return pl.pallas_call(
        functools.partial(route_kernel, owners),
        out_shape=(
            jax.ShapeDtypeStruct((owners, 128), I32),
            jax.ShapeDtypeStruct((total, 128), I32),
        ),
        in_specs=[VMEM] * 4,
        out_specs=(VMEM, VMEM),
        scratch_shapes=[pltpu.VMEM((total, 128), F32), pltpu.VMEM((128, 128), F32)],
        name="route",
    )(hot_row, cold_row, cold_owner, is_cold)


def forward_form(weight, fields, height):
    rows = weight.shape[0]
    maps = weight.shape[1] // fields
    turned = weight.reshape(rows, maps, fields).transpose(0, 2, 1)
    tall = -(-rows // 16) * 16
    padded = jnp.pad(turned, ((0, tall - rows), (0, 0), (0, height - maps)))
    return padded.reshape(tall, fields * height)


def backward_form(weight, fields, height):
    rows = weight.shape[0]
    maps = weight.shape[1] // fields
    turned = weight.reshape(rows, maps, fields).transpose(2, 1, 0)
    padded = jnp.pad(turned, ((0, 0), (0, height - maps), (0, 128 - rows)))
    return padded.reshape(fields * height, 128)


def call_cin(grad_logit, hot_row, is_cold, slot, back, hot_table, out_weight, forward, backward):
    samples, fields = hot_row.shape
    total = samples * FP
    hot_rows, breadth = hot_table.shape
    lanes = samples * breadth
    maps = out_weight.shape[1]
    tall = -(-maps // 16) * 16
    owners, slots = back.shape[0], back.shape[0] * back.shape[1]
    weights_line = jnp.pad(out_weight.T, ((0, tall - maps), (0, 128 - out_weight.shape[0])))
    return pl.pallas_call(
        cin_kernel,
        out_shape=(
            jax.ShapeDtypeStruct((samples,), F32),
            jax.ShapeDtypeStruct((owners, SLOT + hot_rows // owners, breadth), BF16),
        ),
        in_specs=[SMEM] + [VMEM] * 12,
        out_specs=(SMEM, VMEM),
        scratch_shapes=[
            pltpu.VMEM((128, 128), F32),
            pltpu.VMEM((total, hot_rows + slots), BF16),
            pltpu.VMEM((48, lanes), F32),
            pltpu.VMEM((48, lanes), BF16),
            pltpu.VMEM((tall, lanes), BF16),
            pltpu.VMEM((tall, lanes), BF16),
            pltpu.VMEM((tall, lanes), BF16),
            pltpu.VMEM((fields * tall, lanes), BF16),
            pltpu.VMEM((tall, lanes), F32),
            pltpu.VMEM((FP * 8, lanes), F32),
            pltpu.VMEM((tall, lanes), F32),
            pltpu.VMEM((128, lanes), BF16),
        ],
        compiler_params=pltpu.CompilerParams(vmem_limit_bytes=56 << 20),
        name="cin",
    )(
        grad_logit, hot_row, is_cold, slot, back.reshape(slots, breadth), hot_table,
        weights_line, *forward, *backward,
    )


def local(
    hot_row, cold_row, cold_owner, is_cold, grad_logit, hot_table, cold_table,
    first_weight, second_weight, third_weight, out_weight,
):
    samples, fields = hot_row.shape
    breadth = hot_table.shape[1]
    owners = lax.axis_size("shard")
    weights = (first_weight, second_weight, third_weight)
    heights = (48, 112, 112)
    forward = [forward_form(w, fields, h) for w, h in zip(weights, heights)]
    backward = [backward_form(w, fields, h) for w, h in zip(weights, heights)]
    ask, slot = call_route(hot_row, cold_row, cold_owner, is_cold, owners)
    requested = lax.all_to_all(ask[:, :SLOT], "shard", split_axis=0, concat_axis=0, tiled=True)
    found = jnp.take(cold_table, requested, axis=0)
    returned = lax.all_to_all(found, "shard", split_axis=0, concat_axis=0, tiled=True)
    logits, outgoing = call_cin(
        grad_logit, hot_row, is_cold, slot, returned, hot_table, out_weight, forward, backward
    )
    incoming = lax.all_to_all(outgoing, "shard", split_axis=0, concat_axis=0, tiled=True)
    cold_in = incoming[:, :SLOT].astype(F32)
    cold_local = jax.ops.segment_sum(
        cold_in.reshape(-1, breadth), requested.reshape(-1), num_segments=cold_table.shape[0]
    )
    cold_total = lax.psum(cold_local.astype(BF16), "group")
    hot_part = jnp.sum(incoming[:, SLOT:].astype(F32), axis=0).astype(BF16)
    hot_mine = jnp.sum(lax.all_gather(hot_part, "group").astype(F32), axis=0).astype(BF16)
    hot_grad = lax.all_gather(hot_mine, "shard", axis=0, tiled=True)
    return (hot_grad, cold_total, logits)


def solution(mesh):
    across = P(("group", "shard"), None)
    return jax.shard_map(
        local,
        mesh=mesh,
        in_specs=(
            across, across, across, across, P(("group", "shard")), P(), P("shard", None),
            P(), P(), P(), P(),
        ),
        out_specs=(P(), P("shard", None), P(("group", "shard"))),
        check_vma=False,
    )
```

```python
import functools

import jax
import jax.numpy as jnp
from jax import lax
from jax.experimental import pallas as pl
from jax.experimental.pallas import tpu as pltpu
from jax.sharding import PartitionSpec as P

CAP = 9
SLOT = 16
FP = 40
VMEM = pl.BlockSpec(memory_space=pltpu.VMEM)
SMEM = pl.BlockSpec(memory_space=pltpu.SMEM)
F32 = jnp.float32
BF16 = jnp.bfloat16
I32 = jnp.int32


def iota(shape, dim):
    return lax.broadcasted_iota(I32, shape, dim)


def route_kernel(owners, hot_ref, row_ref, owner_ref, cold_ref, ask_ref, slot_ref, want_ref, pad_ref):
    samples, fields = hot_ref.shape
    total = samples * FP
    code = jnp.where(cold_ref[...] == 1, owner_ref[...], -1)
    pad_ref[...] = jnp.full(pad_ref.shape, -1.0, F32)
    pad_ref[0:samples, 0:fields] = code.astype(F32)
    pad_ref[samples : 2 * samples, 0:fields] = row_ref[...].astype(F32)
    pad_ref[2 * samples : 3 * samples, 0:fields] = jnp.where(
        cold_ref[...] == 1, -1, hot_ref[...]
    ).astype(F32)
    turned = pad_ref[...].T
    lane = iota((FP, 128), 1).astype(F32)
    for s in range(samples):
        want_ref[s * FP : (s + 1) * FP, :] = jnp.where(
            turned[0:FP, s : s + 1] == lane, 1.0, 0.0
        )
    wanted = want_ref[...]
    below = (iota((total, total), 0) > iota((total, total), 1)).astype(F32).astype(BF16)
    earlier = jnp.dot(below, wanted.astype(BF16), preferred_element_type=F32)
    position = jnp.sum(earlier * wanted, axis=1, keepdims=True)
    lane_all = iota((total, 128), 1).astype(F32)
    owner_col = jnp.sum(wanted * lane_all, axis=1, keepdims=True)
    is_cold = jnp.sum(wanted, axis=1, keepdims=True)
    slot = jnp.where(is_cold > 0.0, owner_col * SLOT + position, -1.0)
    slot_ref[...] = jnp.broadcast_to(slot, (total, 128)).astype(I32)
    row_col = jnp.concatenate(
        [turned[0:FP, samples + s : samples + s + 1] for s in range(samples)], axis=0
    ).astype(I32)
    at = jnp.broadcast_to(position, (total, 128)) == lane_all
    high = jnp.where(at, (row_col >> 6).astype(F32), 0.0).astype(BF16)
    low = jnp.where(at, (row_col & 63).astype(F32), 0.0).astype(BF16)
    there = jnp.where(at, 1.0, 0.0).astype(BF16)
    turned_want = wanted.T[0:owners, :].astype(BF16)
    asked = jnp.dot(
        turned_want, jnp.concatenate([high, low, there], axis=1), preferred_element_type=F32
    )
    row = asked[:, 0:128] * 64.0 + asked[:, 128:256]
    ask_ref[...] = jnp.where(asked[:, 256:384] > 0.0, row, 0.0).astype(I32)


def cin_kernel(
    gl_ref,
    hot_ref,
    cold_ref,
    slot_ref,
    back_ref,
    table_ref,
    out_weight_ref,
    f1_ref,
    f2_ref,
    f3_ref,
    b1_ref,
    b2_ref,
    b3_ref,
    logit_ref,
    outgoing_ref,
    pad_ref,
    pick_ref,
    emb_ref,
    embb_ref,
    x2_ref,
    x3_ref,
    x4_ref,
    outer_ref,
    carry_ref,
    part_ref,
    pool_ref,
    grad_ref,
):
    samples, fields = hot_ref.shape
    total = samples * FP
    breadth = table_ref.shape[1]
    lanes = samples * breadth
    hot_rows = table_ref.shape[0]
    slots = back_ref.shape[0]
    pad_ref[...] = jnp.full(pad_ref.shape, -1.0, F32)
    pad_ref[0:samples, 0:fields] = jnp.where(cold_ref[...] == 1, -1, hot_ref[...]).astype(F32)
    turned = pad_ref[...].T.astype(I32)
    slot = slot_ref[...]

    for s in range(samples):
        ids = turned[0:FP, s : s + 1]
        pick_ref[s * FP : (s + 1) * FP, 0:hot_rows] = (
            jnp.where(ids == iota((FP, hot_rows), 1), 1.0, 0.0).astype(BF16)
        )
    pick_ref[:, hot_rows : hot_rows + slots] = (
        jnp.where(
            jnp.concatenate([slot] * (slots // 128), axis=1) == iota((total, slots), 1), 1.0, 0.0
        ).astype(BF16)
    )
    rows = jnp.dot(pick_ref[:, 0:hot_rows], table_ref[...], preferred_element_type=F32) + jnp.dot(
        pick_ref[:, hot_rows : hot_rows + slots], back_ref[...], preferred_element_type=F32
    )
    emb_ref[...] = jnp.zeros(emb_ref.shape, F32)
    for s in range(samples):
        emb_ref[0:FP, s * breadth : (s + 1) * breadth] = rows[s * FP : (s + 1) * FP, :]
    embb_ref[...] = emb_ref[...].astype(BF16)

    pool_ref[...] = jnp.zeros(pool_ref.shape, F32)
    states = (embb_ref, x2_ref, x3_ref, x4_ref)
    for k, w_ref in enumerate((f1_ref, f2_ref, f3_ref)):
        source = states[k]
        height = source.shape[0]

        def fill(f, _, source=source, height=height):
            line = jnp.broadcast_to(emb_ref[pl.ds(f, 1), :], (16, lanes)).astype(BF16)
            for r in range(0, height, 16):
                at = pl.multiple_of(f * height + r, 16)
                outer_ref[pl.ds(at, 16), :] = source[r : r + 16, :] * line
            return 0

        lax.fori_loop(0, fields, fill, 0)
        depth = fields * height
        weight = w_ref[...]
        for n in range(0, lanes, 256):
            value = jnp.dot(
                weight, outer_ref[0:depth, n : n + 256], preferred_element_type=F32
            ).astype(BF16)
            states[k + 1][:, n : n + 256] = value
            pool_ref[:, n : n + 256] += value.astype(F32) * out_weight_ref[:, k : k + 1]

    for s in range(samples):
        logit_ref[s] = jnp.sum(pool_ref[:, s * breadth : (s + 1) * breadth])

    part_ref[...] = jnp.zeros(part_ref.shape, F32)
    tall = carry_ref.shape[0]
    grad_ref[...] = jnp.zeros(grad_ref.shape, BF16)
    for k, w_ref in reversed(tuple(enumerate((b1_ref, b2_ref, b3_ref)))):
        source = states[k]
        height = source.shape[0]
        for s in range(samples):
            at = slice(s * breadth, (s + 1) * breadth)
            value = jnp.broadcast_to(gl_ref[s] * out_weight_ref[:, k : k + 1], (tall, breadth))
            if k < 2:
                value = value + carry_ref[:, at]
            grad_ref[0:tall, at] = value.astype(BF16)
        carry_ref[0:height, :] = jnp.zeros((height, lanes), F32)

        def back(f, _, source=source, height=height, w_ref=w_ref):
            at = pl.multiple_of(f * height, 16)
            at8 = pl.multiple_of(f * 8, 8)
            for n in range(0, lanes, 256):
                cols = slice(n, n + 256)
                outer = jnp.dot(
                    w_ref[pl.ds(at, height), :], grad_ref[:, cols], preferred_element_type=F32
                )
                carry_ref[0:height, cols] += outer * emb_ref[pl.ds(f, 1), cols]
                mixed = outer * source[:, cols].astype(F32)
                total_rows = mixed[0:8]
                for r in range(8, height, 8):
                    total_rows = total_rows + mixed[r : r + 8]
                part_ref[pl.ds(at8, 8), cols] += total_rows
            return 0

        lax.fori_loop(0, fields, back, 0)

    grads = carry_ref[0:FP, :] + jnp.sum(part_ref[...].reshape(FP, 8, lanes), axis=1)
    stacked = jnp.concatenate(
        [grads[:, s * breadth : (s + 1) * breadth] for s in range(samples)], axis=0
    ).astype(BF16)
    owners = outgoing_ref.shape[0]
    share = hot_rows // owners
    slot_line = slot.astype(F32).T[0:1].astype(I32)
    hot_col = jnp.concatenate([turned[0:FP, s : s + 1] for s in range(samples)], axis=0)
    hot_wide = jnp.broadcast_to(hot_col, (total, 128)).astype(F32).T[0:1].astype(I32)
    line = jnp.where(jnp.broadcast_to(slot_line, (slots, total)) == iota((slots, total), 0), 1.0, 0.0)
    sent_cold = jnp.dot(line.astype(BF16), stacked, preferred_element_type=F32).astype(BF16)
    line = jnp.where(jnp.broadcast_to(hot_wide, (hot_rows, total)) == iota((hot_rows, total), 0), 1.0, 0.0)
    sent_hot = jnp.dot(line.astype(BF16), stacked, preferred_element_type=F32).astype(BF16)
    outgoing_ref[:, 0:SLOT, :] = sent_cold.reshape(owners, SLOT, breadth)
    outgoing_ref[:, SLOT : SLOT + share, :] = sent_hot.reshape(owners, share, breadth)


def call_route(hot_row, cold_row, cold_owner, is_cold, owners):
    samples, fields = hot_row.shape
    total = samples * FP
    return pl.pallas_call(
        functools.partial(route_kernel, owners),
        out_shape=(
            jax.ShapeDtypeStruct((owners, 128), I32),
            jax.ShapeDtypeStruct((total, 128), I32),
        ),
        in_specs=[VMEM] * 4,
        out_specs=(VMEM, VMEM),
        scratch_shapes=[pltpu.VMEM((total, 128), F32), pltpu.VMEM((128, 128), F32)],
        name="route",
    )(hot_row, cold_row, cold_owner, is_cold)


def forward_form(weight, fields, height):
    rows = weight.shape[0]
    maps = weight.shape[1] // fields
    turned = weight.reshape(rows, maps, fields).transpose(0, 2, 1)
    tall = -(-rows // 16) * 16
    padded = jnp.pad(turned, ((0, tall - rows), (0, 0), (0, height - maps)))
    return padded.reshape(tall, fields * height)


def backward_form(weight, fields, height):
    rows = weight.shape[0]
    maps = weight.shape[1] // fields
    turned = weight.reshape(rows, maps, fields).transpose(2, 1, 0)
    padded = jnp.pad(turned, ((0, 0), (0, height - maps), (0, 128 - rows)))
    return padded.reshape(fields * height, 128)


def call_cin(grad_logit, hot_row, is_cold, slot, back, hot_table, out_weight, forward, backward):
    samples, fields = hot_row.shape
    total = samples * FP
    hot_rows, breadth = hot_table.shape
    lanes = samples * breadth
    maps = out_weight.shape[1]
    tall = -(-maps // 16) * 16
    owners, slots = back.shape[0], back.shape[0] * back.shape[1]
    weights_line = jnp.pad(out_weight.T, ((0, tall - maps), (0, 128 - out_weight.shape[0])))
    return pl.pallas_call(
        cin_kernel,
        out_shape=(
            jax.ShapeDtypeStruct((samples,), F32),
            jax.ShapeDtypeStruct((owners, SLOT + hot_rows // owners, breadth), BF16),
        ),
        in_specs=[SMEM] + [VMEM] * 12,
        out_specs=(SMEM, VMEM),
        scratch_shapes=[
            pltpu.VMEM((128, 128), F32),
            pltpu.VMEM((total, hot_rows + slots), BF16),
            pltpu.VMEM((48, lanes), F32),
            pltpu.VMEM((48, lanes), BF16),
            pltpu.VMEM((tall, lanes), BF16),
            pltpu.VMEM((tall, lanes), BF16),
            pltpu.VMEM((tall, lanes), BF16),
            pltpu.VMEM((fields * tall, lanes), BF16),
            pltpu.VMEM((tall, lanes), F32),
            pltpu.VMEM((FP * 8, lanes), F32),
            pltpu.VMEM((tall, lanes), F32),
            pltpu.VMEM((128, lanes), BF16),
        ],
        compiler_params=pltpu.CompilerParams(vmem_limit_bytes=56 << 20),
        name="cin",
    )(
        grad_logit, hot_row, is_cold, slot, back.reshape(slots, breadth), hot_table,
        weights_line, *forward, *backward,
    )


def merge_kernel(in_ref, ask_ref, out_ref, wide_ref):
    owners = in_ref.shape[0]
    share = in_ref.shape[1] - SLOT
    rows = owners * CAP
    for o in range(owners):
        wide_ref[o * CAP : (o + 1) * CAP, :] = in_ref[o, 0:CAP, :].astype(F32)
    out_ref[0:rows, :] = wide_ref[...].astype(BF16)
    width = 384
    slot = iota((128, width), 1)
    place = (slot * 7282) >> 16
    rest = slot - place * CAP
    spread = jnp.where(rest == iota((128, width), 0), 1.0, 0.0).astype(BF16)
    keep = place[0:owners] == iota((owners, width), 0)
    ask = jnp.concatenate([ask_ref[...] >> 6, ask_ref[...] & 63], axis=0).astype(F32).astype(BF16)
    wide = jnp.dot(ask, spread, preferred_element_type=F32)
    high = jnp.sum(jnp.where(keep, wide[0:owners], 0.0), axis=0, keepdims=True)
    low = jnp.sum(jnp.where(keep, wide[owners:], 0.0), axis=0, keepdims=True)
    lines = [v[:, n : n + 128] for v in (high, low) for n in range(0, width, 128)]
    lines.append(jnp.zeros((2, 128), F32))
    out_ref[rows : rows + 8, :] = jnp.concatenate(lines, axis=0).astype(BF16)
    sums = in_ref[0, SLOT : SLOT + share, :].astype(F32)
    for o in range(1, owners):
        sums = sums + in_ref[o, SLOT : SLOT + share, :].astype(F32)
    out_ref[rows + 8 : rows + 8 + share, :] = sums.astype(BF16)


def hot_kernel(height, *refs):
    parts, out_ref = refs[:-1], refs[-1]
    owners, share, breadth = out_ref.shape
    sums = jnp.zeros((share, breadth), F32)
    for part in parts:
        for top in range(0, part.shape[0], height):
            sums = sums + part[top + height - share : top + height, :].astype(F32)
    value = sums.astype(BF16)
    for o in range(owners):
        out_ref[o] = value


def scatter_kernel(height, rows, *refs):
    parts, out_ref, stack_ref, line_ref, pick_ref = refs[:-4], *refs[-4:]
    width = 384
    count = 0
    stack_ref[...] = jnp.zeros(stack_ref.shape, BF16)
    for part in parts:
        for top in range(0, part.shape[0], height):
            stack_ref[count * width : count * width + rows, :] = part[top : top + rows, :]
            ids = part[top + rows : top + rows + 8, :].astype(F32).astype(I32)
            for n in range(3):
                at = slice(count * width + n * 128, count * width + (n + 1) * 128)
                line_ref[:, at] = jnp.broadcast_to(ids[n : n + 1] * 64 + ids[n + 3 : n + 4], (8, 128))
            count += 1
    depth = count * width
    block = pick_ref.shape[0]

    def step(b, _):
        base = b * block
        for n in range(0, depth, 128):
            line = jnp.broadcast_to(line_ref[0:1, n : n + 128], (block, 128))
            pick_ref[:, n : n + 128] = jnp.where(
                line == base + iota((block, 128), 0), 1.0, 0.0
            ).astype(BF16)
        out_ref[pl.ds(pl.multiple_of(base, block), block), :] = jnp.dot(
            pick_ref[...], stack_ref[...], preferred_element_type=F32
        ).astype(BF16)
        return 0

    lax.fori_loop(0, out_ref.shape[0] // block, step, 0)


def call_merge(incoming, requested):
    owners, tall, breadth = incoming.shape
    height = owners * CAP + 8 + tall - SLOT
    return pl.pallas_call(
        merge_kernel,
        out_shape=jax.ShapeDtypeStruct((height, breadth), BF16),
        in_specs=[VMEM, VMEM],
        out_specs=VMEM,
        scratch_shapes=[pltpu.VMEM((owners * CAP, breadth), F32)],
        name="merge",
    )(incoming, requested)


def call_hot(parts, height, owners, share):
    breadth = parts[0].shape[1]
    return pl.pallas_call(
        functools.partial(hot_kernel, height),
        out_shape=jax.ShapeDtypeStruct((owners, share, breadth), BF16),
        in_specs=[VMEM] * len(parts),
        out_specs=VMEM,
        name="hot_sum",
    )(*parts)


def call_scatter(parts, height, rows, table_rows):
    breadth = parts[0].shape[1]
    count = sum(part.shape[0] for part in parts) // height
    block = 256
    return pl.pallas_call(
        functools.partial(scatter_kernel, height, rows),
        out_shape=jax.ShapeDtypeStruct((table_rows, breadth), BF16),
        in_specs=[VMEM] * len(parts),
        out_specs=VMEM,
        scratch_shapes=[
            pltpu.VMEM((count * 384, breadth), BF16),
            pltpu.VMEM((8, count * 384), I32),
            pltpu.VMEM((block, count * 384), BF16),
        ],
        name="cold_scatter",
    )(*parts)


def exchange(block):
    groups = lax.axis_size("group")
    half = groups // 2

    def move(x, hop):
        return lax.ppermute(x, "group", [(i, (i + hop) % groups) for i in range(groups)])

    pair = jnp.concatenate([block, move(block, half)], axis=0)
    parts = [pair]
    up = down = pair
    for hop in range(1, half):
        if hop % 2 == 1:
            up = move(up, 1)
            parts.append(up)
        else:
            down = move(down, -1)
            parts.append(down)
    return parts


def local(
    hot_row, cold_row, cold_owner, is_cold, grad_logit, hot_table, cold_table,
    first_weight, second_weight, third_weight, out_weight,
):
    samples, fields = hot_row.shape
    breadth = hot_table.shape[1]
    owners = lax.axis_size("shard")
    weights = (first_weight, second_weight, third_weight)
    heights = (48, 112, 112)
    forward = [forward_form(w, fields, h) for w, h in zip(weights, heights)]
    backward = [backward_form(w, fields, h) for w, h in zip(weights, heights)]
    ask, slot = call_route(hot_row, cold_row, cold_owner, is_cold, owners)
    ask_in = lax.all_to_all(ask, "shard", split_axis=0, concat_axis=0, tiled=True)
    requested = ask_in[:, :SLOT]
    found = jnp.take(cold_table, requested, axis=0)
    returned = lax.all_to_all(found, "shard", split_axis=0, concat_axis=0, tiled=True)
    logits, outgoing = call_cin(
        grad_logit, hot_row, is_cold, slot, returned, hot_table, out_weight, forward, backward
    )
    incoming = lax.all_to_all(outgoing, "shard", split_axis=0, concat_axis=0, tiled=True)
    block = call_merge(incoming, ask_in)
    rows = owners * CAP
    share = hot_table.shape[0] // owners
    height = block.shape[0]
    parts = exchange(block)
    hot_out = lax.all_to_all(
        call_hot(parts, height, owners, share), "shard", split_axis=0, concat_axis=0, tiled=True
    )
    cold_total = call_scatter(parts, height, rows, cold_table.shape[0])
    hot_grad = hot_out.reshape(hot_table.shape)
    return (hot_grad, cold_total, logits)


def solution(mesh):
    across = P(("group", "shard"), None)
    return jax.shard_map(
        local,
        mesh=mesh,
        in_specs=(
            across, across, across, across, P(("group", "shard")), P(), P("shard", None),
            P(), P(), P(), P(),
        ),
        out_specs=(P(), P("shard", None), P(("group", "shard"))),
        check_vma=False,
    )
```

```python
import functools

import jax
import jax.numpy as jnp
from jax import lax
from jax.experimental import pallas as pl
from jax.experimental.pallas import tpu as pltpu
from jax.sharding import PartitionSpec as P

CAP = 9
SLOT = 16
FP = 40
GROUP = 3
VMEM = pl.BlockSpec(memory_space=pltpu.VMEM)
HBM = pl.BlockSpec(memory_space=pltpu.HBM)
SMEM = pl.BlockSpec(memory_space=pltpu.SMEM)
F32 = jnp.float32
BF16 = jnp.bfloat16
I32 = jnp.int32


def iota(shape, dim):
    return lax.broadcasted_iota(I32, shape, dim)


def route_kernel(owners, hot_ref, row_ref, owner_ref, cold_ref, ask_ref, slot_ref, want_ref, pad_ref):
    samples, fields = hot_ref.shape
    total = samples * FP
    code = jnp.where(cold_ref[...] == 1, owner_ref[...], -1)
    pad_ref[...] = jnp.full(pad_ref.shape, -1.0, F32)
    pad_ref[0:samples, 0:fields] = code.astype(F32)
    pad_ref[samples : 2 * samples, 0:fields] = row_ref[...].astype(F32)
    pad_ref[2 * samples : 3 * samples, 0:fields] = jnp.where(
        cold_ref[...] == 1, -1, hot_ref[...]
    ).astype(F32)
    turned = pad_ref[...].T
    lane = iota((FP, 128), 1).astype(F32)
    for s in range(samples):
        want_ref[s * FP : (s + 1) * FP, :] = jnp.where(
            turned[0:FP, s : s + 1] == lane, 1.0, 0.0
        )
    wanted = want_ref[...]
    below = (iota((total, total), 0) > iota((total, total), 1)).astype(F32).astype(BF16)
    earlier = jnp.dot(below, wanted.astype(BF16), preferred_element_type=F32)
    position = jnp.sum(earlier * wanted, axis=1, keepdims=True)
    lane_all = iota((total, 128), 1).astype(F32)
    owner_col = jnp.sum(wanted * lane_all, axis=1, keepdims=True)
    is_cold = jnp.sum(wanted, axis=1, keepdims=True)
    slot = jnp.where(is_cold > 0.0, owner_col * SLOT + position, -1.0)
    slot_ref[...] = jnp.broadcast_to(slot, (total, 128)).astype(I32)
    row_col = jnp.concatenate(
        [turned[0:FP, samples + s : samples + s + 1] for s in range(samples)], axis=0
    ).astype(I32)
    at = jnp.broadcast_to(position, (total, 128)) == lane_all
    high = jnp.where(at, (row_col >> 6).astype(F32), 0.0).astype(BF16)
    low = jnp.where(at, (row_col & 63).astype(F32), 0.0).astype(BF16)
    there = jnp.where(at, 1.0, 0.0).astype(BF16)
    turned_want = wanted.T[0:owners, :].astype(BF16)
    asked = jnp.dot(
        turned_want, jnp.concatenate([high, low, there], axis=1), preferred_element_type=F32
    )
    row = asked[:, 0:128] * 64.0 + asked[:, 128:256]
    ask_ref[...] = jnp.where(asked[:, 256:384] > 0.0, row, 0.0).astype(I32)


def cin_kernel(
    gl_ref,
    hot_ref,
    cold_ref,
    slot_ref,
    back_ref,
    out_weight_ref,
    table_hbm,
    f1_hbm,
    f2_hbm,
    f3_hbm,
    b1_hbm,
    b2_hbm,
    b3_hbm,
    logit_ref,
    outgoing_ref,
    pad_ref,
    pick_ref,
    emb_ref,
    embb_ref,
    x2_ref,
    x3_ref,
    w2_ref,
    w3_ref,
    outer_ref,
    carry_ref,
    part_ref,
    pool_ref,
    grad_ref,
    table_ref,
    f1_ref,
    f2_ref,
    f3_ref,
    b1_ref,
    b2_ref,
    b3_ref,
    sems,
):
    held = (table_ref, f1_ref, f2_ref, f3_ref, b3_ref, b2_ref, b1_ref)
    kept = (table_hbm, f1_hbm, f2_hbm, f3_hbm, b3_hbm, b2_hbm, b1_hbm)
    copies = [
        pltpu.make_async_copy(source, target, sems.at[n])
        for n, (source, target) in enumerate(zip(kept, held))
    ]
    for copy in copies:
        copy.start()
    samples, fields = hot_ref.shape
    total = samples * FP
    breadth = table_ref.shape[1]
    lanes = samples * breadth
    hot_rows = table_ref.shape[0]
    slots = back_ref.shape[0]
    pad_ref[...] = jnp.full(pad_ref.shape, -1.0, F32)
    pad_ref[0:samples, 0:fields] = jnp.where(cold_ref[...] == 1, -1, hot_ref[...]).astype(F32)
    turned = pad_ref[...].T.astype(I32)
    slot = slot_ref[...]

    for s in range(samples):
        ids = turned[0:FP, s : s + 1]
        pick_ref[s * FP : (s + 1) * FP, 0:hot_rows] = (
            jnp.where(ids == iota((FP, hot_rows), 1), 1.0, 0.0).astype(BF16)
        )
    pick_ref[:, hot_rows : hot_rows + slots] = (
        jnp.where(
            jnp.concatenate([slot] * (slots // 128), axis=1) == iota((total, slots), 1), 1.0, 0.0
        ).astype(BF16)
    )
    copies[0].wait()
    rows = jnp.dot(pick_ref[:, 0:hot_rows], table_ref[...], preferred_element_type=F32) + jnp.dot(
        pick_ref[:, hot_rows : hot_rows + slots], back_ref[...], preferred_element_type=F32
    )
    emb_ref[...] = jnp.zeros(emb_ref.shape, F32)
    for s in range(samples):
        emb_ref[0:FP, s * breadth : (s + 1) * breadth] = rows[s * FP : (s + 1) * FP, :]
    embb_ref[...] = emb_ref[...].astype(BF16)

    pool_ref[...] = jnp.zeros(pool_ref.shape, F32)
    states = (embb_ref, x2_ref, x3_ref)
    wides = (emb_ref, w2_ref, w3_ref)
    for k, w_ref in enumerate((f1_ref, f2_ref, f3_ref)):
        source = states[k]
        height = source.shape[0]

        def fill(f, _, source=source, height=height):
            line = jnp.broadcast_to(emb_ref[pl.ds(f, 1), :], (16, lanes)).astype(BF16)
            for r in range(0, height, 16):
                at = pl.multiple_of(f * height + r, 16)
                outer_ref[pl.ds(at, 16), :] = source[r : r + 16, :] * line
            return 0

        lax.fori_loop(0, fields, fill, 0)
        depth = fields * height
        copies[1 + k].wait()
        weight = w_ref[...]
        for n in range(0, lanes, 256):
            value = jnp.dot(
                weight, outer_ref[0:depth, n : n + 256], preferred_element_type=F32
            ).astype(BF16)
            wide = value.astype(F32)
            if k < 2:
                states[k + 1][:, n : n + 256] = value
                wides[k + 1][:, n : n + 256] = wide
            pool_ref[:, n : n + 256] += wide * out_weight_ref[:, k : k + 1]

    for s in range(samples):
        logit_ref[s] = jnp.sum(pool_ref[:, s * breadth : (s + 1) * breadth])

    part_ref[...] = jnp.zeros(part_ref.shape, F32)
    tall = carry_ref.shape[0]
    grad_ref[...] = jnp.zeros(grad_ref.shape, BF16)
    for k, w_ref in reversed(tuple(enumerate((b1_ref, b2_ref, b3_ref)))):
        copies[6 - k].wait()
        source = wides[k]
        height = source.shape[0]
        for s in range(samples):
            at = slice(s * breadth, (s + 1) * breadth)
            value = jnp.broadcast_to(gl_ref[s] * out_weight_ref[:, k : k + 1], (tall, breadth))
            if k < 2:
                value = value + carry_ref[:, at]
            grad_ref[0:tall, at] = value.astype(BF16)
        carry_ref[0:height, :] = jnp.zeros((height, lanes), F32)

        def back(t, _, source=source, height=height, w_ref=w_ref):
            at = pl.multiple_of(t * (GROUP * height), 16)
            at8 = pl.multiple_of(t * (GROUP * 8), 8)
            for n in range(0, lanes, 256):
                cols = slice(n, n + 256)
                outer = jnp.dot(
                    w_ref[pl.ds(at, GROUP * height), :],
                    grad_ref[:, cols],
                    preferred_element_type=F32,
                )
                sums = [None] * GROUP
                lines = [
                    jnp.broadcast_to(emb_ref[pl.ds(t * GROUP + u, 1), cols], (8, 256))
                    for u in range(GROUP)
                ]
                for r in range(0, height, 8):
                    value = source[r : r + 8, cols]
                    total_rows = carry_ref[r : r + 8, cols]
                    for u in range(GROUP):
                        piece = outer[u * height + r : u * height + r + 8]
                        total_rows = total_rows + piece * lines[u]
                        mixed = piece * value
                        sums[u] = mixed if r == 0 else sums[u] + mixed
                    carry_ref[r : r + 8, cols] = total_rows
                for u in range(GROUP):
                    part_ref[pl.ds(at8 + u * 8, 8), cols] += sums[u]
            return 0

        lax.fori_loop(0, fields // GROUP, back, 0)

    grads = carry_ref[0:FP, :] + jnp.sum(part_ref[...].reshape(FP, 8, lanes), axis=1)
    stacked = jnp.concatenate(
        [grads[:, s * breadth : (s + 1) * breadth] for s in range(samples)], axis=0
    ).astype(BF16)
    owners = outgoing_ref.shape[0]
    share = hot_rows // owners
    slot_line = slot.astype(F32).T[0:1].astype(I32)
    hot_col = jnp.concatenate([turned[0:FP, s : s + 1] for s in range(samples)], axis=0)
    hot_wide = jnp.broadcast_to(hot_col, (total, 128)).astype(F32).T[0:1].astype(I32)
    line = jnp.where(jnp.broadcast_to(slot_line, (slots, total)) == iota((slots, total), 0), 1.0, 0.0)
    sent_cold = jnp.dot(line.astype(BF16), stacked, preferred_element_type=F32).astype(BF16)
    line = jnp.where(jnp.broadcast_to(hot_wide, (hot_rows, total)) == iota((hot_rows, total), 0), 1.0, 0.0)
    sent_hot = jnp.dot(line.astype(BF16), stacked, preferred_element_type=F32).astype(BF16)
    outgoing_ref[:, 0:SLOT, :] = sent_cold.reshape(owners, SLOT, breadth)
    outgoing_ref[:, SLOT : SLOT + share, :] = sent_hot.reshape(owners, share, breadth)


def call_route(hot_row, cold_row, cold_owner, is_cold, owners):
    samples, fields = hot_row.shape
    total = samples * FP
    return pl.pallas_call(
        functools.partial(route_kernel, owners),
        out_shape=(
            jax.ShapeDtypeStruct((owners, 128), I32),
            jax.ShapeDtypeStruct((total, 128), I32),
        ),
        in_specs=[VMEM] * 4,
        out_specs=(VMEM, VMEM),
        scratch_shapes=[pltpu.VMEM((total, 128), F32), pltpu.VMEM((128, 128), F32)],
        compiler_params=pltpu.CompilerParams(vmem_limit_bytes=4 << 20),
        name="route",
    )(hot_row, cold_row, cold_owner, is_cold)


def prep_kernel(fields, *refs):
    count = (len(refs) - 3) // 5
    weights, outs = refs[0:count], refs[count : 3 * count]
    held, (line_ref, wide_ref, sems) = refs[3 * count : 5 * count], refs[5 * count :]
    copies = []
    for k, w_ref in enumerate(weights):
        f_ref, b_ref = held[2 * k : 2 * k + 2]
        rows, cols = w_ref.shape
        pitch = b_ref.shape[0] // fields
        line_ref[...] = jnp.zeros(line_ref.shape, F32)
        line_ref[0:rows, 0:cols] = w_ref[...].astype(F32)
        for c in range(0, fields * pitch, 128):
            if c < cols:
                wide_ref[c : c + 128, :] = line_ref[:, c : c + 128].T
            else:
                wide_ref[c : c + 128, :] = jnp.zeros((128, 128), F32)
        for f in range(fields):
            b_ref[f * pitch : (f + 1) * pitch, :] = wide_ref[
                pl.ds(f, pitch, stride=fields), :
            ].astype(BF16)
        copies.append(pltpu.make_async_copy(b_ref, outs[2 * k + 1], sems.at[2 * k + 1]))
        copies[-1].start()
        tall = f_ref.shape[0]
        for c in range(0, fields * pitch, 128):
            width = min(128, fields * pitch - c)
            f_ref[:, c : c + width] = b_ref[c : c + width, :].T[0:tall]
        copies.append(pltpu.make_async_copy(f_ref, outs[2 * k], sems.at[2 * k]))
        copies[-1].start()
    for copy in copies:
        copy.wait()


def call_prep(weights, fields):
    rows = weights[0].shape[0]
    tall = -(-rows // 16) * 16
    shapes = []
    for w in weights:
        pitch = -(-(w.shape[1] // fields) // 16) * 16
        shapes.append(jax.ShapeDtypeStruct((tall, fields * pitch), BF16))
        shapes.append(jax.ShapeDtypeStruct((fields * pitch, 128), BF16))
    deep = max(-(-shape.shape[0] // 128) * 128 for shape in shapes)
    return pl.pallas_call(
        functools.partial(prep_kernel, fields),
        out_shape=tuple(pltpu.HBM(shape.shape, BF16) for shape in shapes),
        in_specs=[VMEM] * len(weights),
        out_specs=tuple([HBM] * len(shapes)),
        scratch_shapes=[pltpu.VMEM(shape.shape, BF16) for shape in shapes]
        + [
            pltpu.VMEM((128, deep), F32),
            pltpu.VMEM((deep, 128), F32),
            pltpu.SemaphoreType.DMA((len(shapes),)),
        ],
        compiler_params=pltpu.CompilerParams(vmem_limit_bytes=14 << 20),
        name="prep",
    )(*weights)


def call_cin(grad_logit, hot_row, is_cold, slot, back, hot_table, out_weight, forward, backward):
    samples, fields = hot_row.shape
    total = samples * FP
    hot_rows, breadth = hot_table.shape
    lanes = samples * breadth
    maps = out_weight.shape[1]
    tall = -(-maps // 16) * 16
    owners, slots = back.shape[0], back.shape[0] * back.shape[1]
    weights_line = jnp.pad(out_weight.T, ((0, tall - maps), (0, 128 - out_weight.shape[0])))
    return pl.pallas_call(
        cin_kernel,
        out_shape=(
            jax.ShapeDtypeStruct((samples,), F32),
            jax.ShapeDtypeStruct((owners, SLOT + hot_rows // owners, breadth), BF16),
        ),
        in_specs=[SMEM] + [VMEM] * 5 + [HBM] * 7,
        out_specs=(SMEM, VMEM),
        scratch_shapes=[
            pltpu.VMEM((128, 128), F32),
            pltpu.VMEM((total, hot_rows + slots), BF16),
            pltpu.VMEM((48, lanes), F32),
            pltpu.VMEM((48, lanes), BF16),
            pltpu.VMEM((tall, lanes), BF16),
            pltpu.VMEM((tall, lanes), BF16),
            pltpu.VMEM((tall, lanes), F32),
            pltpu.VMEM((tall, lanes), F32),
            pltpu.VMEM((fields * tall, lanes), BF16),
            pltpu.VMEM((tall, lanes), F32),
            pltpu.VMEM((FP * 8, lanes), F32),
            pltpu.VMEM((tall, lanes), F32),
            pltpu.VMEM((128, lanes), BF16),
        ]
        + [pltpu.VMEM(x.shape, BF16) for x in (hot_table, *forward, *backward)]
        + [pltpu.SemaphoreType.DMA((7,))],
        compiler_params=pltpu.CompilerParams(vmem_limit_bytes=32 << 20),
        name="cin",
    )(
        grad_logit, hot_row, is_cold, slot, back.reshape(slots, breadth),
        weights_line,
        *(pltpu.with_memory_space_constraint(x, pltpu.HBM) for x in (hot_table, *forward, *backward)),
    )


def merge_kernel(in_ref, ask_ref, out_ref, wide_ref):
    owners = in_ref.shape[0]
    share = in_ref.shape[1] - SLOT
    rows = owners * CAP
    for o in range(owners):
        wide_ref[o * CAP : (o + 1) * CAP, :] = in_ref[o, 0:CAP, :].astype(F32)
    out_ref[0:rows, :] = wide_ref[...].astype(BF16)
    width = 384
    slot = iota((128, width), 1)
    slot = jnp.where(slot < 256, slot, 256 + (slot & 31))
    place = (slot * 7282) >> 16
    rest = slot - place * CAP
    spread = jnp.where(rest == iota((128, width), 0), 1.0, 0.0).astype(BF16)
    keep = place[0:owners] == iota((owners, width), 0)
    ask = jnp.concatenate([ask_ref[...] >> 8, ask_ref[...] & 255], axis=0).astype(F32).astype(BF16)
    wide = jnp.dot(ask, spread, preferred_element_type=F32)
    high = jnp.sum(jnp.where(keep, wide[0:owners], 0.0), axis=0, keepdims=True)
    low = jnp.sum(jnp.where(keep, wide[owners:], 0.0), axis=0, keepdims=True)
    lines = [v[:, n : n + 128] for v in (high, low) for n in range(0, width, 128)]
    lines.append(jnp.zeros((2, 128), F32))
    out_ref[rows : rows + 8, :] = jnp.concatenate(lines, axis=0).astype(BF16)
    sums = in_ref[0, SLOT : SLOT + share, :].astype(F32)
    for o in range(1, owners):
        sums = sums + in_ref[o, SLOT : SLOT + share, :].astype(F32)
    out_ref[rows + 8 : rows + 8 + share, :] = sums.astype(BF16)


def hot_kernel(height, *refs):
    parts, out_ref = refs[:-1], refs[-1]
    owners, share, breadth = out_ref.shape
    sums = jnp.zeros((share, breadth), F32)
    for part in parts:
        for top in range(0, part.shape[0], height):
            sums = sums + part[top + height - share : top + height, :].astype(F32)
    value = sums.astype(BF16)
    for o in range(owners):
        out_ref[o] = value


def scatter_kernel(height, rows, *refs):
    parts, out_ref, stack_ref, high_ref, low_ref, pick_ref, wide_ref, rhs_ref = refs[:-7], *refs[-7:]
    full = rows // 128 * 128
    tail = rows - full
    per = 128 // tail
    sources = [(part, top) for part in parts for top in range(0, part.shape[0], height)]
    deep = len(sources) * full
    lane = iota((16, 128), 1)
    lines = len(sources) // per
    for n, (part, top) in enumerate(sources):
        stack_ref[n * full : (n + 1) * full, :] = part[top : top + full, :]
        at = deep + n * tail
        stack_ref[at : at + tail, :] = part[top + full : top + rows, :]
    for half, line_ref in ((0, high_ref), (3, low_ref)):
        for n, (part, top) in enumerate(sources):
            ids = part[top + rows : top + rows + 8, :].astype(F32)
            for c in range(full // 128):
                at = n * full + c * 128
                line_ref[:, at : at + 128] = jnp.broadcast_to(
                    ids[half + c : half + c + 1], (16, 128)
                ).astype(BF16)
        for t in range(lines):
            merged = jnp.zeros((16, 128), F32)
            for u in range(per):
                part, top = sources[t * per + u]
                row = part[top + rows : top + rows + 8, :].astype(F32)[half + 2 : half + 3]
                merged = jnp.where(lane // tail == u, jnp.broadcast_to(row, (16, 128)), merged)
            at = deep + t * 128
            line_ref[:, at : at + 128] = merged.astype(BF16)
    depth = stack_ref.shape[0]
    block = pick_ref.shape[0]
    one = jnp.ones((16, 128), BF16)
    zero = jnp.zeros((16, 128), BF16)
    for r in range(0, block, 16):
        place = (iota((16, 128), 0) + r).astype(F32).astype(BF16)
        for n in range(0, depth, 128):
            pick_ref[r : r + 16, n : n + 128] = jnp.where(low_ref[:, n : n + 128] == place, one, zero)
    for n in range(0, depth, 128):
        wide_ref[n : n + 128, :] = (
            jnp.broadcast_to(high_ref[0:1, n : n + 128].astype(F32), (128, 128)).T.astype(BF16)
        )

    def step(t, _):
        for u in range(2):
            for v in range(2):
                mine = jnp.full((16, 128), 4 * t + 2 * u + v, I32).astype(F32).astype(BF16)
                for n in range(0, depth, 16):
                    rhs_ref[u, n : n + 16, v * 128 : (v + 1) * 128] = jnp.where(
                        wide_ref[n : n + 16, :] == mine, stack_ref[n : n + 16, :], zero
                    )
            value = jnp.dot(pick_ref[...], rhs_ref[u], preferred_element_type=F32).astype(BF16)
            for v in range(2):
                at = pl.multiple_of((4 * t + 2 * u + v) * block, block)
                out_ref[pl.ds(at, block), :] = value[:, v * 128 : (v + 1) * 128]
        return 0

    lax.fori_loop(0, out_ref.shape[0] // block // 4, step, 0)


def call_merge(incoming, requested):
    owners, tall, breadth = incoming.shape
    height = owners * CAP + 8 + tall - SLOT
    return pl.pallas_call(
        merge_kernel,
        out_shape=jax.ShapeDtypeStruct((height, breadth), BF16),
        in_specs=[VMEM, VMEM],
        out_specs=VMEM,
        scratch_shapes=[pltpu.VMEM((owners * CAP, breadth), F32)],
        compiler_params=pltpu.CompilerParams(vmem_limit_bytes=4 << 20),
        name="merge",
    )(incoming, requested)


def call_hot(parts, height, owners, share):
    breadth = parts[0].shape[1]
    return pl.pallas_call(
        functools.partial(hot_kernel, height),
        out_shape=jax.ShapeDtypeStruct((owners, share, breadth), BF16),
        in_specs=[VMEM] * len(parts),
        out_specs=VMEM,
        compiler_params=pltpu.CompilerParams(vmem_limit_bytes=4 << 20),
        name="hot_sum",
    )(*parts)


def call_scatter(parts, height, rows, table_rows):
    breadth = parts[0].shape[1]
    count = sum(part.shape[0] for part in parts) // height
    block = 256
    return pl.pallas_call(
        functools.partial(scatter_kernel, height, rows),
        out_shape=jax.ShapeDtypeStruct((table_rows, breadth), BF16),
        in_specs=[VMEM] * len(parts),
        out_specs=VMEM,
        scratch_shapes=[
            pltpu.VMEM((count * rows, breadth), BF16),
            pltpu.VMEM((16, count * rows), BF16),
            pltpu.VMEM((16, count * rows), BF16),
            pltpu.VMEM((block, count * rows), BF16),
            pltpu.VMEM((count * rows, breadth), BF16),
            pltpu.VMEM((2, count * rows, 2 * breadth), BF16),
        ],
        compiler_params=pltpu.CompilerParams(vmem_limit_bytes=16 << 20),
        name="cold_scatter",
    )(*parts)


def exchange(block):
    groups = lax.axis_size("group")
    half = groups // 2

    def move(x, hop):
        return lax.ppermute(x, "group", [(i, (i + hop) % groups) for i in range(groups)])

    pair = jnp.concatenate([block, move(block, half)], axis=0)
    parts = [pair]
    up = down = pair
    for hop in range(1, half):
        if hop % 2 == 1:
            up = move(up, 1)
            parts.append(up)
        else:
            down = move(down, -1)
            parts.append(down)
    return parts


def local(
    hot_row, cold_row, cold_owner, is_cold, grad_logit, hot_table, cold_table,
    first_weight, second_weight, third_weight, out_weight,
):
    samples, fields = hot_row.shape
    breadth = hot_table.shape[1]
    owners = lax.axis_size("shard")
    forms = call_prep((first_weight, second_weight, third_weight), fields)
    ask, slot = call_route(hot_row, cold_row, cold_owner, is_cold, owners)
    ask_in = lax.all_to_all(ask, "shard", split_axis=0, concat_axis=0, tiled=True)
    requested = ask_in[:, :SLOT]
    found = jnp.take(cold_table, requested, axis=0)
    returned = lax.all_to_all(found, "shard", split_axis=0, concat_axis=0, tiled=True)
    logits, outgoing = call_cin(
        grad_logit, hot_row, is_cold, slot, returned, hot_table, out_weight, forms[0::2], forms[1::2]
    )
    incoming = lax.all_to_all(outgoing, "shard", split_axis=0, concat_axis=0, tiled=True)
    block = call_merge(incoming, ask_in)
    rows = owners * CAP
    share = hot_table.shape[0] // owners
    height = block.shape[0]
    parts = exchange(block)
    hot_out = lax.all_to_all(
        call_hot(parts, height, owners, share), "shard", split_axis=0, concat_axis=0, tiled=True
    )
    cold_total = call_scatter(parts, height, rows, cold_table.shape[0])
    hot_grad = hot_out.reshape(hot_table.shape)
    return (hot_grad, cold_total, logits)


def solution(mesh):
    across = P(("group", "shard"), None)
    return jax.shard_map(
        local,
        mesh=mesh,
        in_specs=(
            across, across, across, across, P(("group", "shard")), P(), P("shard", None),
            P(), P(), P(), P(),
        ),
        out_specs=(P(), P("shard", None), P(("group", "shard"))),
        check_vma=False,
    )
```

```python
import functools

import jax
import jax.numpy as jnp
from jax import lax
from jax.experimental import pallas as pl
from jax.experimental.pallas import tpu as pltpu
from jax.sharding import PartitionSpec as P

CAP = 9
SLOT = 16
FP = 40
GROUP = 3
VMEM = pl.BlockSpec(memory_space=pltpu.VMEM)
HBM = pl.BlockSpec(memory_space=pltpu.HBM)
SMEM = pl.BlockSpec(memory_space=pltpu.SMEM)
F32 = jnp.float32
BF16 = jnp.bfloat16
I32 = jnp.int32


def iota(shape, dim):
    return lax.broadcasted_iota(I32, shape, dim)


def route_kernel(
    owners, row_hbm, owner_hbm, cold_hbm, ask_ref, slot_ref, want_ref, pad_ref,
    row_ref, owner_ref, cold_ref, sems,
):
    copies = [
        pltpu.make_async_copy(source, target, sems.at[n])
        for n, (source, target) in enumerate(
            ((row_hbm, row_ref), (owner_hbm, owner_ref), (cold_hbm, cold_ref))
        )
    ]
    for copy in copies:
        copy.start()
    for copy in copies:
        copy.wait()
    samples, fields = row_ref.shape
    total = samples * FP
    code = jnp.where(cold_ref[...] == 1, owner_ref[...], -1)
    pad_ref[...] = jnp.full(pad_ref.shape, -1.0, F32)
    pad_ref[0:samples, 0:fields] = code.astype(F32)
    pad_ref[samples : 2 * samples, 0:fields] = row_ref[...].astype(F32)
    turned = pad_ref[...].T
    lane = iota((FP, 128), 1).astype(F32)
    for s in range(samples):
        want_ref[s * FP : (s + 1) * FP, :] = jnp.where(
            turned[0:FP, s : s + 1] == lane, 1.0, 0.0
        )
    wanted = want_ref[...]
    below = (iota((total, total), 0) > iota((total, total), 1)).astype(F32).astype(BF16)
    earlier = jnp.dot(below, wanted.astype(BF16), preferred_element_type=F32)
    position = jnp.sum(earlier * wanted, axis=1, keepdims=True)
    lane_all = iota((total, 128), 1).astype(F32)
    owner_col = jnp.sum(wanted * lane_all, axis=1, keepdims=True)
    is_cold = jnp.sum(wanted, axis=1, keepdims=True)
    slot = jnp.where(is_cold > 0.0, owner_col * SLOT + position, -1.0)
    slot_ref[...] = jnp.broadcast_to(slot, (total, 128)).astype(I32)
    row_col = jnp.concatenate(
        [turned[0:FP, samples + s : samples + s + 1] for s in range(samples)], axis=0
    ).astype(I32)
    at = jnp.broadcast_to(position, (total, 128)) == lane_all
    high = jnp.where(at, (row_col >> 6).astype(F32), 0.0).astype(BF16)
    low = jnp.where(at, (row_col & 63).astype(F32), 0.0).astype(BF16)
    there = jnp.where(at, 1.0, 0.0).astype(BF16)
    turned_want = wanted.T[0:owners, :].astype(BF16)
    asked = jnp.dot(
        turned_want, jnp.concatenate([high, low, there], axis=1), preferred_element_type=F32
    )
    row = asked[:, 0:128] * 64.0 + asked[:, 128:256]
    ask_ref[...] = jnp.where(asked[:, 256:384] > 0.0, row, 0.0).astype(I32)


def cin_kernel(
    gl_ref,
    hot_ref,
    hot_line_ref,
    slot_ref,
    back_ref,
    scale_ref,
    f1_hbm,
    f2_hbm,
    f3_hbm,
    b1_hbm,
    b2_hbm,
    b3_hbm,
    logit_ref,
    outgoing_ref,
    pick_ref,
    out_weight_ref,
    emb_ref,
    embb_ref,
    x2_ref,
    x3_ref,
    w2_ref,
    w3_ref,
    outer_ref,
    carry_ref,
    part_ref,
    pool_ref,
    grad_ref,
    f1_ref,
    f2_ref,
    f3_ref,
    b1_ref,
    b2_ref,
    b3_ref,
    sems,
):
    held = (f1_ref, f2_ref, f3_ref, b3_ref, b2_ref, b1_ref)
    kept = (f1_hbm, f2_hbm, f3_hbm, b3_hbm, b2_hbm, b1_hbm)
    copies = [
        pltpu.make_async_copy(source, target, sems.at[n])
        for n, (source, target) in enumerate(zip(kept, held))
    ]
    for copy in copies:
        copy.start()
    samples = gl_ref.shape[0]
    total, breadth = hot_ref.shape
    fields = b1_ref.shape[0] // embb_ref.shape[0]
    lanes = samples * breadth
    slots = back_ref.shape[0]
    owners = outgoing_ref.shape[0]
    share = outgoing_ref.shape[1] - SLOT
    hot_rows = owners * share
    slot = slot_ref[...]
    layers, maps = scale_ref.shape
    tall = carry_ref.shape[0]
    out_weight_ref[...] = jnp.zeros(out_weight_ref.shape, F32)
    out_weight_ref[0:layers, 0:maps] = scale_ref[...]
    out_weight_ref[...] = out_weight_ref[...].T

    for n in range(0, slots, 128):
        pick_ref[:, n : n + 128] = jnp.where(
            slot == iota((total, 128), 1) + n, 1.0, 0.0
        ).astype(BF16)
    rows = hot_ref[...].astype(F32) + jnp.dot(
        pick_ref[...], back_ref[...], preferred_element_type=F32
    )
    emb_ref[...] = jnp.zeros(emb_ref.shape, F32)
    for s in range(samples):
        emb_ref[0:FP, s * breadth : (s + 1) * breadth] = rows[s * FP : (s + 1) * FP, :]
    embb_ref[...] = emb_ref[...].astype(BF16)

    pool_ref[...] = jnp.zeros(pool_ref.shape, F32)
    states = (embb_ref, x2_ref, x3_ref)
    wides = (emb_ref, w2_ref, w3_ref)
    for k, w_ref in enumerate((f1_ref, f2_ref, f3_ref)):
        source = states[k]
        height = source.shape[0]

        def fill(f, _, source=source, height=height):
            line = jnp.broadcast_to(emb_ref[pl.ds(f, 1), :], (16, lanes)).astype(BF16)
            for r in range(0, height, 16):
                at = pl.multiple_of(f * height + r, 16)
                outer_ref[pl.ds(at, 16), :] = source[r : r + 16, :] * line
            return 0

        lax.fori_loop(0, fields, fill, 0)
        depth = fields * height
        copies[k].wait()
        weight = w_ref[...]
        for n in range(0, lanes, 256):
            value = jnp.dot(
                weight, outer_ref[0:depth, n : n + 256], preferred_element_type=F32
            ).astype(BF16)
            wide = value.astype(F32)
            if k < 2:
                states[k + 1][:, n : n + 256] = value
                wides[k + 1][:, n : n + 256] = wide
            pool_ref[:, n : n + 256] += wide * out_weight_ref[0:tall, k : k + 1]

    for s in range(samples):
        logit_ref[s] = jnp.sum(pool_ref[:, s * breadth : (s + 1) * breadth])

    part_ref[...] = jnp.zeros(part_ref.shape, F32)
    grad_ref[...] = jnp.zeros(grad_ref.shape, BF16)
    for k, w_ref in reversed(tuple(enumerate((b1_ref, b2_ref, b3_ref)))):
        copies[5 - k].wait()
        source = wides[k]
        height = source.shape[0]
        for s in range(samples):
            at = slice(s * breadth, (s + 1) * breadth)
            value = jnp.broadcast_to(gl_ref[s] * out_weight_ref[0:tall, k : k + 1], (tall, breadth))
            if k < 2:
                value = value + carry_ref[:, at]
            grad_ref[0:tall, at] = value.astype(BF16)
        carry_ref[0:height, :] = jnp.zeros((height, lanes), F32)

        def back(n, _, source=source, height=height, w_ref=w_ref):
            cols = pl.ds(pl.multiple_of(n * 256, 256), 256)
            for t in range(0, fields, GROUP):
                outer = jnp.dot(
                    w_ref[t * height : (t + GROUP) * height, :],
                    grad_ref[:, cols],
                    preferred_element_type=F32,
                )
                sums = [None] * GROUP
                lines = [
                    jnp.broadcast_to(emb_ref[t + u : t + u + 1, cols], (8, 256))
                    for u in range(GROUP)
                ]
                for r in range(0, height, 8):
                    value = source[r : r + 8, cols]
                    total_rows = carry_ref[r : r + 8, cols]
                    for u in range(GROUP):
                        piece = outer[u * height + r : u * height + r + 8]
                        total_rows = total_rows + piece * lines[u]
                        mixed = piece * value
                        sums[u] = mixed if r == 0 else sums[u] + mixed
                    carry_ref[r : r + 8, cols] = total_rows
                for u in range(GROUP):
                    part_ref[(t + u) * 8 : (t + u + 1) * 8, cols] += sums[u]
            return 0

        lax.fori_loop(0, lanes // 256, back, 0)

    grads = carry_ref[0:FP, :] + jnp.sum(part_ref[...].reshape(FP, 8, lanes), axis=1)
    stacked = jnp.concatenate(
        [grads[:, s * breadth : (s + 1) * breadth] for s in range(samples)], axis=0
    ).astype(BF16)
    slot_line = slot.astype(F32).T[0:1].astype(I32)
    hot_wide = hot_line_ref[0:1]
    line = jnp.where(jnp.broadcast_to(slot_line, (slots, total)) == iota((slots, total), 0), 1.0, 0.0)
    sent_cold = jnp.dot(line.astype(BF16), stacked, preferred_element_type=F32).astype(BF16)
    line = jnp.where(jnp.broadcast_to(hot_wide, (hot_rows, total)) == iota((hot_rows, total), 0), 1.0, 0.0)
    sent_hot = jnp.dot(line.astype(BF16), stacked, preferred_element_type=F32).astype(BF16)
    outgoing_ref[:, 0:SLOT, :] = sent_cold.reshape(owners, SLOT, breadth)
    outgoing_ref[:, SLOT : SLOT + share, :] = sent_hot.reshape(owners, share, breadth)


def call_route(cold_row, cold_owner, is_cold, owners):
    samples, fields = cold_row.shape
    total = samples * FP
    return pl.pallas_call(
        functools.partial(route_kernel, owners),
        out_shape=(
            jax.ShapeDtypeStruct((owners, 128), I32),
            jax.ShapeDtypeStruct((total, 128), I32),
        ),
        in_specs=[HBM] * 3,
        out_specs=(VMEM, VMEM),
        scratch_shapes=[pltpu.VMEM((total, 128), F32), pltpu.VMEM((128, 128), F32)]
        + [pltpu.VMEM((samples, fields), I32)] * 3
        + [pltpu.SemaphoreType.DMA((3,))],
        compiler_params=pltpu.CompilerParams(vmem_limit_bytes=4 << 20),
        name="route",
    )(*(pltpu.with_memory_space_constraint(x, pltpu.HBM) for x in (cold_row, cold_owner, is_cold)))


def hot_rows_kernel(hot_ref, cold_ref, table_ref, rows_ref, line_ref, pad_ref, pick_ref):
    samples, fields = hot_ref.shape
    total = samples * FP
    hot_rows = table_ref.shape[0]
    pad_ref[...] = jnp.full(pad_ref.shape, -1.0, F32)
    pad_ref[0:samples, 0:fields] = jnp.where(cold_ref[...] == 1, -1, hot_ref[...]).astype(F32)
    turned = pad_ref[...].T
    for s in range(samples):
        ids = turned[0:FP, s : s + 1].astype(I32)
        pick_ref[s * FP : (s + 1) * FP, :] = jnp.where(
            ids == iota((FP, hot_rows), 1), 1.0, 0.0
        ).astype(BF16)
    rows_ref[...] = jnp.dot(
        pick_ref[...], table_ref[...], preferred_element_type=F32
    ).astype(BF16)
    hot_col = jnp.concatenate([turned[0:FP, s : s + 1] for s in range(samples)], axis=0)
    line_ref[...] = jnp.broadcast_to(hot_col, (total, 128)).T[0:8].astype(I32)


def call_hot_rows(hot_row, is_cold, hot_table):
    samples, fields = hot_row.shape
    total = samples * FP
    return pl.pallas_call(
        hot_rows_kernel,
        out_shape=(
            jax.ShapeDtypeStruct((total, hot_table.shape[1]), BF16),
            jax.ShapeDtypeStruct((8, total), I32),
        ),
        in_specs=[VMEM] * 3,
        out_specs=(VMEM, VMEM),
        scratch_shapes=[
            pltpu.VMEM((128, 128), F32),
            pltpu.VMEM((total, hot_table.shape[0]), BF16),
        ],
        compiler_params=pltpu.CompilerParams(vmem_limit_bytes=6 << 20),
        name="hot_rows",
    )(hot_row, is_cold, hot_table)


def prep_kernel(fields, *refs):
    count = (len(refs) - 3) // 5
    weights, outs = refs[0:count], refs[count : 3 * count]
    held, (line_ref, wide_ref, sems) = refs[3 * count : 5 * count], refs[5 * count :]
    copies = []
    for k, w_ref in enumerate(weights):
        f_ref, b_ref = held[2 * k : 2 * k + 2]
        rows, cols = w_ref.shape
        pitch = b_ref.shape[0] // fields
        line_ref[...] = jnp.zeros(line_ref.shape, F32)
        line_ref[0:rows, 0:cols] = w_ref[...].astype(F32)
        for c in range(0, fields * pitch, 128):
            if c < cols:
                wide_ref[c : c + 128, :] = line_ref[:, c : c + 128].T
            else:
                wide_ref[c : c + 128, :] = jnp.zeros((128, 128), F32)
        for f in range(fields):
            b_ref[f * pitch : (f + 1) * pitch, :] = wide_ref[
                pl.ds(f, pitch, stride=fields), :
            ].astype(BF16)
        copies.append(pltpu.make_async_copy(b_ref, outs[2 * k + 1], sems.at[2 * k + 1]))
        copies[-1].start()
        tall = f_ref.shape[0]
        for c in range(0, fields * pitch, 128):
            width = min(128, fields * pitch - c)
            f_ref[:, c : c + width] = b_ref[c : c + width, :].T[0:tall]
        copies.append(pltpu.make_async_copy(f_ref, outs[2 * k], sems.at[2 * k]))
        copies[-1].start()
    for copy in copies:
        copy.wait()


def call_prep(weights, fields):
    rows = weights[0].shape[0]
    tall = -(-rows // 16) * 16
    shapes = []
    for w in weights:
        pitch = -(-(w.shape[1] // fields) // 16) * 16
        shapes.append(jax.ShapeDtypeStruct((tall, fields * pitch), BF16))
        shapes.append(jax.ShapeDtypeStruct((fields * pitch, 128), BF16))
    deep = max(-(-shape.shape[0] // 128) * 128 for shape in shapes)
    return pl.pallas_call(
        functools.partial(prep_kernel, fields),
        out_shape=tuple(pltpu.HBM(shape.shape, BF16) for shape in shapes),
        in_specs=[VMEM] * len(weights),
        out_specs=tuple([HBM] * len(shapes)),
        scratch_shapes=[pltpu.VMEM(shape.shape, BF16) for shape in shapes]
        + [
            pltpu.VMEM((128, deep), F32),
            pltpu.VMEM((deep, 128), F32),
            pltpu.SemaphoreType.DMA((len(shapes),)),
        ],
        compiler_params=pltpu.CompilerParams(vmem_limit_bytes=14 << 20),
        name="prep",
    )(*weights)


def call_cin(grad_logit, hot_values, hot_line, slot, back, hot_rows, out_weight, forward, backward):
    total, breadth = hot_values.shape
    samples = grad_logit.shape[0]
    lanes = samples * breadth
    owners, slots = back.shape[0], back.shape[0] * back.shape[1]
    tall = forward[0].shape[0]
    small = -(-(FP) // 16) * 16
    fields = backward[0].shape[0] // small
    return pl.pallas_call(
        cin_kernel,
        out_shape=(
            jax.ShapeDtypeStruct((samples,), F32),
            jax.ShapeDtypeStruct((owners, SLOT + hot_rows // owners, breadth), BF16),
        ),
        in_specs=[SMEM] + [VMEM] * 5 + [HBM] * 6,
        out_specs=(SMEM, VMEM),
        scratch_shapes=[
            pltpu.VMEM((total, slots), BF16),
            pltpu.VMEM((128, 128), F32),
            pltpu.VMEM((small, lanes), F32),
            pltpu.VMEM((small, lanes), BF16),
            pltpu.VMEM((tall, lanes), BF16),
            pltpu.VMEM((tall, lanes), BF16),
            pltpu.VMEM((tall, lanes), F32),
            pltpu.VMEM((tall, lanes), F32),
            pltpu.VMEM((fields * tall, lanes), BF16),
            pltpu.VMEM((tall, lanes), F32),
            pltpu.VMEM((FP * 8, lanes), F32),
            pltpu.VMEM((tall, lanes), F32),
            pltpu.VMEM((128, lanes), BF16),
        ]
        + [pltpu.VMEM(x.shape, BF16) for x in (*forward, *backward)]
        + [pltpu.SemaphoreType.DMA((6,))],
        compiler_params=pltpu.CompilerParams(vmem_limit_bytes=32 << 20),
        name="cin",
    )(
        grad_logit, hot_values, hot_line, slot, back.reshape(slots, breadth), out_weight,
        *(pltpu.with_memory_space_constraint(x, pltpu.HBM) for x in (*forward, *backward)),
    )


def merge_kernel(in_ref, ask_ref, out_ref, wide_ref):
    owners = in_ref.shape[0]
    share = in_ref.shape[1] - SLOT
    rows = owners * CAP
    for o in range(owners):
        wide_ref[o * CAP : (o + 1) * CAP, :] = in_ref[o, 0:CAP, :].astype(F32)
    value = wide_ref[...].astype(BF16)
    copies = out_ref.shape[0]
    for c in range(copies):
        out_ref[c, 0:rows, :] = value
    width = 384
    slot = iota((128, width), 1)
    slot = jnp.where(slot < 256, slot, 256 + (slot & 31))
    place = (slot * 7282) >> 16
    rest = slot - place * CAP
    spread = jnp.where(rest == iota((128, width), 0), 1.0, 0.0).astype(BF16)
    keep = place[0:owners] == iota((owners, width), 0)
    ask = jnp.concatenate([ask_ref[...] >> 8, ask_ref[...] & 255], axis=0).astype(F32).astype(BF16)
    wide = jnp.dot(ask, spread, preferred_element_type=F32)
    high = jnp.sum(jnp.where(keep, wide[0:owners], 0.0), axis=0, keepdims=True)
    low = jnp.sum(jnp.where(keep, wide[owners:], 0.0), axis=0, keepdims=True)
    lines = [v[:, n : n + 128] for v in (high, low) for n in range(0, width, 128)]
    lines.append(jnp.zeros((2, 128), F32))
    value = jnp.concatenate(lines, axis=0).astype(BF16)
    for c in range(copies):
        out_ref[c, rows : rows + 8, :] = value
    sums = in_ref[0, SLOT : SLOT + share, :].astype(F32)
    for o in range(1, owners):
        sums = sums + in_ref[o, SLOT : SLOT + share, :].astype(F32)
    value = sums.astype(BF16)
    for c in range(copies):
        out_ref[c, rows + 8 : rows + 8 + share, :] = value


def pack_kernel(rows, in_ref, out_ref):
    count, height = in_ref.shape[0:2]
    sums = in_ref[0, rows:height, :].astype(F32)
    out_ref[0:rows, :] = in_ref[0, 0:rows, :]
    for c in range(1, count):
        out_ref[c * rows : (c + 1) * rows, :] = in_ref[c, 0:rows, :]
        sums = sums + in_ref[c, rows:height, :].astype(F32)
    out_ref[count * rows :, :] = sums.astype(BF16)


def hot_kernel(*refs):
    parts, out_ref = refs[:-1], refs[-1]
    owners, share, breadth = out_ref.shape
    sums = jnp.zeros((share, breadth), F32)
    for part in parts:
        top = part.shape[0] - share
        sums = sums + part[top : top + share, :].astype(F32)
    value = sums.astype(BF16)
    for o in range(owners):
        out_ref[o] = value


def scatter_kernel(height, rows, *refs):
    parts, out_ref, stack_ref, high_ref, low_ref, pick_ref, wide_ref, rhs_ref = refs[:-7], *refs[-7:]
    full = rows // 128 * 128
    tail = rows - full
    per = 128 // tail
    sources = [
        (part, top)
        for part in parts
        for top in range(0, part.shape[0] // height * height, height)
    ]
    deep = len(sources) * full
    lane = iota((16, 128), 1)
    lines = len(sources) // per
    for n, (part, top) in enumerate(sources):
        stack_ref[n * full : (n + 1) * full, :] = part[top : top + full, :]
        at = deep + n * tail
        stack_ref[at : at + tail, :] = part[top + full : top + rows, :]
    for half, line_ref in ((0, high_ref), (3, low_ref)):
        for n, (part, top) in enumerate(sources):
            ids = part[top + rows : top + rows + 8, :].astype(F32)
            for c in range(full // 128):
                at = n * full + c * 128
                line_ref[:, at : at + 128] = jnp.broadcast_to(
                    ids[half + c : half + c + 1], (16, 128)
                ).astype(BF16)
        for t in range(lines):
            merged = jnp.zeros((16, 128), F32)
            for u in range(per):
                part, top = sources[t * per + u]
                row = part[top + rows : top + rows + 8, :].astype(F32)[half + 2 : half + 3]
                merged = jnp.where(lane // tail == u, jnp.broadcast_to(row, (16, 128)), merged)
            at = deep + t * 128
            line_ref[:, at : at + 128] = merged.astype(BF16)
    depth = stack_ref.shape[0]
    block = pick_ref.shape[0]
    one = jnp.ones((16, 128), BF16)
    zero = jnp.zeros((16, 128), BF16)
    for r in range(0, block, 16):
        place = (iota((16, 128), 0) + r).astype(F32).astype(BF16)
        for n in range(0, depth, 128):
            pick_ref[r : r + 16, n : n + 128] = jnp.where(low_ref[:, n : n + 128] == place, one, zero)
    for n in range(0, depth, 128):
        wide_ref[n : n + 128, :] = (
            jnp.broadcast_to(high_ref[0:1, n : n + 128].astype(F32), (128, 128)).T.astype(BF16)
        )

    def step(t, _):
        for u in range(2):
            for v in range(2):
                mine = jnp.full((16, 128), 4 * t + 2 * u + v, I32).astype(F32).astype(BF16)
                for n in range(0, depth, 16):
                    rhs_ref[u, n : n + 16, v * 128 : (v + 1) * 128] = jnp.where(
                        wide_ref[n : n + 16, :] == mine, stack_ref[n : n + 16, :], zero
                    )
            value = jnp.dot(pick_ref[...], rhs_ref[u], preferred_element_type=F32).astype(BF16)
            for v in range(2):
                at = pl.multiple_of((4 * t + 2 * u + v) * block, block)
                out_ref[pl.ds(at, block), :] = value[:, v * 128 : (v + 1) * 128]
        return 0

    lax.fori_loop(0, out_ref.shape[0] // block // 4, step, 0)


def call_merge(incoming, requested, copies):
    owners, tall, breadth = incoming.shape
    height = owners * CAP + 8 + tall - SLOT
    return pl.pallas_call(
        merge_kernel,
        out_shape=jax.ShapeDtypeStruct((copies, height, breadth), BF16),
        in_specs=[VMEM, VMEM],
        out_specs=VMEM,
        scratch_shapes=[pltpu.VMEM((owners * CAP, breadth), F32)],
        compiler_params=pltpu.CompilerParams(vmem_limit_bytes=4 << 20),
        name="merge",
    )(incoming, requested)


def call_pack(blocks, rows):
    count, height, breadth = blocks.shape
    return pl.pallas_call(
        functools.partial(pack_kernel, rows),
        out_shape=jax.ShapeDtypeStruct((count * rows + height - rows, breadth), BF16),
        in_specs=[VMEM],
        out_specs=VMEM,
        compiler_params=pltpu.CompilerParams(vmem_limit_bytes=4 << 20),
        name="pack",
    )(blocks)


def call_hot(parts, owners, share):
    breadth = parts[0].shape[1]
    return pl.pallas_call(
        hot_kernel,
        out_shape=jax.ShapeDtypeStruct((owners, share, breadth), BF16),
        in_specs=[VMEM] * len(parts),
        out_specs=VMEM,
        compiler_params=pltpu.CompilerParams(vmem_limit_bytes=6 << 20),
        name="hot_sum",
    )(*parts)


def call_scatter(parts, height, rows, table_rows):
    breadth = parts[0].shape[1]
    count = sum(part.shape[0] // height for part in parts)
    block = 256
    return pl.pallas_call(
        functools.partial(scatter_kernel, height, rows),
        out_shape=jax.ShapeDtypeStruct((table_rows, breadth), BF16),
        in_specs=[VMEM] * len(parts),
        out_specs=VMEM,
        scratch_shapes=[
            pltpu.VMEM((count * rows, breadth), BF16),
            pltpu.VMEM((16, count * rows), BF16),
            pltpu.VMEM((16, count * rows), BF16),
            pltpu.VMEM((block, count * rows), BF16),
            pltpu.VMEM((count * rows, breadth), BF16),
            pltpu.VMEM((2, count * rows, 2 * breadth), BF16),
        ],
        compiler_params=pltpu.CompilerParams(vmem_limit_bytes=16 << 20),
        name="cold_scatter",
    )(*parts)


def exchange(blocks, rows):
    groups = lax.axis_size("group")
    count = blocks.shape[0]
    apart = groups // count

    def move(x, hop):
        return lax.ppermute(x, "group", [(i, (i + hop) % groups) for i in range(groups)])

    classes = [[a + apart * i for i in range(count)] for a in range(apart)]
    mine = call_pack(
        lax.all_to_all(
            blocks, "group", split_axis=0, concat_axis=0, axis_index_groups=classes, tiled=True
        ),
        rows,
    )
    up, down = move(mine, 1), move(mine, -1)
    half = count // 2 * rows
    return mine, up, down, move(up[:half], 1), move(down[half:], -1)


def local(
    hot_row, cold_row, cold_owner, is_cold, grad_logit, hot_table, cold_table,
    first_weight, second_weight, third_weight, out_weight,
):
    samples, fields = hot_row.shape
    breadth = hot_table.shape[1]
    owners = lax.axis_size("shard")
    forms = call_prep((first_weight, second_weight, third_weight), fields)
    ask, slot = call_route(cold_row, cold_owner, is_cold, owners)
    hot_values, hot_line = call_hot_rows(hot_row, is_cold, hot_table)
    ask_in = lax.all_to_all(ask, "shard", split_axis=0, concat_axis=0, tiled=True)
    requested = ask_in[:, :SLOT]
    found = jnp.take(cold_table, requested, axis=0)
    returned = lax.all_to_all(found, "shard", split_axis=0, concat_axis=0, tiled=True)
    logits, outgoing = call_cin(
        grad_logit, hot_values, hot_line, slot, returned, hot_table.shape[0], out_weight,
        forms[0::2], forms[1::2],
    )
    incoming = lax.all_to_all(outgoing, "shard", split_axis=0, concat_axis=0, tiled=True)
    rows = owners * CAP
    share = hot_table.shape[0] // owners
    parts = exchange(call_merge(incoming, ask_in, 4), rows + 8)
    hot_out = lax.all_to_all(
        call_hot((*parts[0:3], parts[4]), owners, share),
        "shard", split_axis=0, concat_axis=0, tiled=True,
    )
    cold_total = call_scatter(parts, rows + 8, rows, cold_table.shape[0])
    hot_grad = hot_out.reshape(hot_table.shape)
    return (hot_grad, cold_total, logits)


def solution(mesh):
    across = P(("group", "shard"), None)
    return jax.shard_map(
        local,
        mesh=mesh,
        in_specs=(
            across, across, across, across, P(("group", "shard")), P(), P("shard", None),
            P(), P(), P(), P(),
        ),
        out_specs=(P(), P("shard", None), P(("group", "shard"))),
        check_vma=False,
    )
```

```python
import functools

import jax
import jax.numpy as jnp
from jax import lax
from jax.experimental import pallas as pl
from jax.experimental.pallas import tpu as pltpu
from jax.sharding import PartitionSpec as P

CAP = 9
SLOT = 16
FP = 40
GROUP = 3
VMEM = pl.BlockSpec(memory_space=pltpu.VMEM)
HBM = pl.BlockSpec(memory_space=pltpu.HBM)
SMEM = pl.BlockSpec(memory_space=pltpu.SMEM)
F32 = jnp.float32
BF16 = jnp.bfloat16
I32 = jnp.int32


def iota(shape, dim):
    return lax.broadcasted_iota(I32, shape, dim)


def route_kernel(
    owners, row_hbm, owner_hbm, cold_hbm, ask_ref, slot_ref, want_ref, pad_ref,
    row_ref, owner_ref, cold_ref, sems,
):
    copies = [
        pltpu.make_async_copy(source, target, sems.at[n])
        for n, (source, target) in enumerate(
            ((row_hbm, row_ref), (owner_hbm, owner_ref), (cold_hbm, cold_ref))
        )
    ]
    for copy in copies:
        copy.start()
    for copy in copies:
        copy.wait()
    samples, fields = row_ref.shape
    total = samples * FP
    code = jnp.where(cold_ref[...] == 1, owner_ref[...], -1)
    pad_ref[...] = jnp.full(pad_ref.shape, -1.0, F32)
    pad_ref[0:samples, 0:fields] = code.astype(F32)
    pad_ref[samples : 2 * samples, 0:fields] = row_ref[...].astype(F32)
    turned = pad_ref[...].T
    lane = iota((FP, 128), 1).astype(F32)
    for s in range(samples):
        want_ref[s * FP : (s + 1) * FP, :] = jnp.where(
            turned[0:FP, s : s + 1] == lane, 1.0, 0.0
        )
    wanted = want_ref[...]
    below = (iota((total, total), 0) > iota((total, total), 1)).astype(F32).astype(BF16)
    earlier = jnp.dot(below, wanted.astype(BF16), preferred_element_type=F32)
    position = jnp.sum(earlier * wanted, axis=1, keepdims=True)
    lane_all = iota((total, 128), 1).astype(F32)
    owner_col = jnp.sum(wanted * lane_all, axis=1, keepdims=True)
    is_cold = jnp.sum(wanted, axis=1, keepdims=True)
    slot = jnp.where(is_cold > 0.0, owner_col * SLOT + position, -1.0)
    slot_ref[...] = jnp.broadcast_to(slot, (total, 128)).astype(I32)
    row_col = jnp.concatenate(
        [turned[0:FP, samples + s : samples + s + 1] for s in range(samples)], axis=0
    ).astype(I32)
    at = jnp.broadcast_to(position, (total, 128)) == lane_all
    high = jnp.where(at, (row_col >> 6).astype(F32), 0.0).astype(BF16)
    low = jnp.where(at, (row_col & 63).astype(F32), 0.0).astype(BF16)
    there = jnp.where(at, 1.0, 0.0).astype(BF16)
    turned_want = wanted.T[0:owners, :].astype(BF16)
    asked = jnp.dot(
        turned_want, jnp.concatenate([high, low, there], axis=1), preferred_element_type=F32
    )
    row = asked[:, 0:128] * 64.0 + asked[:, 128:256]
    ask_ref[...] = jnp.where(asked[:, 256:384] > 0.0, row, 0.0).astype(I32)


def cin_kernel(
    gl_ref,
    hot_line_ref,
    slot_ref,
    back_ref,
    scale_ref,
    hot_hbm,
    f1_hbm,
    f2_hbm,
    f3_hbm,
    b1_hbm,
    b2_hbm,
    b3_hbm,
    logit_ref,
    outgoing_ref,
    pick_ref,
    out_weight_ref,
    emb_ref,
    embb_ref,
    x2_ref,
    x3_ref,
    w2_ref,
    w3_ref,
    outer_ref,
    carry_ref,
    part_ref,
    pool_ref,
    grad_ref,
    f1_ref,
    f2_ref,
    f3_ref,
    b1_ref,
    b2_ref,
    b3_ref,
    hot_ref,
    sems,
):
    held = (hot_ref, f1_ref, f2_ref, f3_ref, b3_ref, b2_ref, b1_ref)
    kept = (hot_hbm, f1_hbm, f2_hbm, f3_hbm, b3_hbm, b2_hbm, b1_hbm)
    copies = [
        pltpu.make_async_copy(source, target, sems.at[n])
        for n, (source, target) in enumerate(zip(kept, held))
    ]
    for copy in copies:
        copy.start()
    samples = gl_ref.shape[0]
    total, breadth = hot_ref.shape
    fields = b1_ref.shape[0] // embb_ref.shape[0]
    lanes = samples * breadth
    slots = back_ref.shape[0]
    owners = outgoing_ref.shape[0]
    share = outgoing_ref.shape[1] - SLOT
    hot_rows = owners * share
    slot = slot_ref[...]
    layers, maps = scale_ref.shape
    tall = carry_ref.shape[0]
    out_weight_ref[...] = jnp.zeros(out_weight_ref.shape, F32)
    out_weight_ref[0:layers, 0:maps] = scale_ref[...]
    out_weight_ref[...] = out_weight_ref[...].T

    for n in range(0, slots, 128):
        pick_ref[:, n : n + 128] = jnp.where(
            slot == iota((total, 128), 1) + n, 1.0, 0.0
        ).astype(BF16)
    copies[0].wait()
    rows = hot_ref[...].astype(F32) + jnp.dot(
        pick_ref[...], back_ref[...], preferred_element_type=F32
    )
    emb_ref[...] = jnp.zeros(emb_ref.shape, F32)
    for s in range(samples):
        emb_ref[0:FP, s * breadth : (s + 1) * breadth] = rows[s * FP : (s + 1) * FP, :]
    embb_ref[...] = emb_ref[...].astype(BF16)

    pool_ref[...] = jnp.zeros(pool_ref.shape, F32)
    states = (embb_ref, x2_ref, x3_ref)
    wides = (emb_ref, w2_ref, w3_ref)
    for k, w_ref in enumerate((f1_ref, f2_ref, f3_ref)):
        source = states[k]
        height = source.shape[0]

        def fill(f, _, source=source, height=height):
            line = jnp.broadcast_to(emb_ref[pl.ds(f, 1), :], (16, lanes)).astype(BF16)
            for r in range(0, height, 16):
                at = pl.multiple_of(f * height + r, 16)
                outer_ref[pl.ds(at, 16), :] = source[r : r + 16, :] * line
            return 0

        lax.fori_loop(0, fields, fill, 0)
        depth = fields * height
        copies[1 + k].wait()
        weight = w_ref[...]
        for n in range(0, lanes, 256):
            value = jnp.dot(
                weight, outer_ref[0:depth, n : n + 256], preferred_element_type=F32
            ).astype(BF16)
            wide = value.astype(F32)
            if k < 2:
                states[k + 1][:, n : n + 256] = value
                wides[k + 1][:, n : n + 256] = wide
            pool_ref[:, n : n + 256] += wide * out_weight_ref[0:tall, k : k + 1]

    for s in range(samples):
        logit_ref[s] = jnp.sum(pool_ref[:, s * breadth : (s + 1) * breadth])

    part_ref[...] = jnp.zeros(part_ref.shape, F32)
    grad_ref[...] = jnp.zeros(grad_ref.shape, BF16)
    for k, w_ref in reversed(tuple(enumerate((b1_ref, b2_ref, b3_ref)))):
        copies[6 - k].wait()
        source = wides[k]
        height = source.shape[0]
        for s in range(samples):
            at = slice(s * breadth, (s + 1) * breadth)
            value = jnp.broadcast_to(gl_ref[s] * out_weight_ref[0:tall, k : k + 1], (tall, breadth))
            if k < 2:
                value = value + carry_ref[:, at]
            grad_ref[0:tall, at] = value.astype(BF16)
        carry_ref[0:height, :] = jnp.zeros((height, lanes), F32)

        def back(n, _, source=source, height=height, w_ref=w_ref):
            cols = pl.ds(pl.multiple_of(n * 256, 256), 256)
            for t in range(0, fields, GROUP):
                outer = jnp.dot(
                    w_ref[t * height : (t + GROUP) * height, :],
                    grad_ref[:, cols],
                    preferred_element_type=F32,
                )
                sums = [None] * GROUP
                lines = [
                    jnp.broadcast_to(emb_ref[t + u : t + u + 1, cols], (8, 256))
                    for u in range(GROUP)
                ]
                for r in range(0, height, 8):
                    value = source[r : r + 8, cols]
                    total_rows = carry_ref[r : r + 8, cols]
                    for u in range(GROUP):
                        piece = outer[u * height + r : u * height + r + 8]
                        total_rows = total_rows + piece * lines[u]
                        mixed = piece * value
                        sums[u] = mixed if r == 0 else sums[u] + mixed
                    carry_ref[r : r + 8, cols] = total_rows
                for u in range(GROUP):
                    part_ref[(t + u) * 8 : (t + u + 1) * 8, cols] += sums[u]
            return 0

        lax.fori_loop(0, lanes // 256, back, 0)

    grads = carry_ref[0:FP, :] + jnp.sum(part_ref[...].reshape(FP, 8, lanes), axis=1)
    stacked = jnp.concatenate(
        [grads[:, s * breadth : (s + 1) * breadth] for s in range(samples)], axis=0
    ).astype(BF16)
    slot_line = slot.astype(F32).T[0:1].astype(I32)
    hot_wide = hot_line_ref[0:1]
    line = jnp.where(jnp.broadcast_to(slot_line, (slots, total)) == iota((slots, total), 0), 1.0, 0.0)
    sent_cold = jnp.dot(line.astype(BF16), stacked, preferred_element_type=F32).astype(BF16)
    line = jnp.where(jnp.broadcast_to(hot_wide, (hot_rows, total)) == iota((hot_rows, total), 0), 1.0, 0.0)
    sent_hot = jnp.dot(line.astype(BF16), stacked, preferred_element_type=F32).astype(BF16)
    outgoing_ref[:, 0:SLOT, :] = sent_cold.reshape(owners, SLOT, breadth)
    outgoing_ref[:, SLOT : SLOT + share, :] = sent_hot.reshape(owners, share, breadth)


def call_route(cold_row, cold_owner, is_cold, owners):
    samples, fields = cold_row.shape
    total = samples * FP
    return pl.pallas_call(
        functools.partial(route_kernel, owners),
        out_shape=(
            jax.ShapeDtypeStruct((owners, 128), I32),
            jax.ShapeDtypeStruct((total, 128), I32),
        ),
        in_specs=[HBM] * 3,
        out_specs=(VMEM, VMEM),
        scratch_shapes=[pltpu.VMEM((total, 128), F32), pltpu.VMEM((128, 128), F32)]
        + [pltpu.VMEM((samples, fields), I32)] * 3
        + [pltpu.SemaphoreType.DMA((3,))],
        compiler_params=pltpu.CompilerParams(vmem_limit_bytes=4 << 20),
        name="route",
    )(*(pltpu.with_memory_space_constraint(x, pltpu.HBM) for x in (cold_row, cold_owner, is_cold)))


def hot_rows_kernel(
    hot_ref, cold_ref, table_ref, rows_hbm, line_ref, pad_ref, pick_ref, rows_ref, sem
):
    samples, fields = hot_ref.shape
    total = samples * FP
    hot_rows = table_ref.shape[0]
    pad_ref[...] = jnp.full(pad_ref.shape, -1.0, F32)
    pad_ref[0:samples, 0:fields] = jnp.where(cold_ref[...] == 1, -1, hot_ref[...]).astype(F32)
    turned = pad_ref[...].T
    for s in range(samples):
        ids = turned[0:FP, s : s + 1].astype(I32)
        pick_ref[s * FP : (s + 1) * FP, :] = jnp.where(
            ids == iota((FP, hot_rows), 1), 1.0, 0.0
        ).astype(BF16)
    rows_ref[...] = jnp.dot(
        pick_ref[...], table_ref[...], preferred_element_type=F32
    ).astype(BF16)
    copy = pltpu.make_async_copy(rows_ref, rows_hbm, sem)
    copy.start()
    hot_col = jnp.concatenate([turned[0:FP, s : s + 1] for s in range(samples)], axis=0)
    line_ref[...] = jnp.broadcast_to(hot_col, (total, 128)).T[0:8].astype(I32)
    copy.wait()


def call_hot_rows(hot_row, is_cold, hot_table):
    samples, fields = hot_row.shape
    total = samples * FP
    return pl.pallas_call(
        hot_rows_kernel,
        out_shape=(
            pltpu.HBM((total, hot_table.shape[1]), BF16),
            jax.ShapeDtypeStruct((8, total), I32),
        ),
        in_specs=[VMEM] * 3,
        out_specs=(HBM, VMEM),
        scratch_shapes=[
            pltpu.VMEM((128, 128), F32),
            pltpu.VMEM((total, hot_table.shape[0]), BF16),
            pltpu.VMEM((total, hot_table.shape[1]), BF16),
            pltpu.SemaphoreType.DMA,
        ],
        compiler_params=pltpu.CompilerParams(vmem_limit_bytes=6 << 20),
        name="hot_rows",
    )(hot_row, is_cold, hot_table)


def prep_kernel(fields, *refs):
    count = (len(refs) - 3) // 5
    weights, outs = refs[0:count], refs[count : 3 * count]
    held, (line_ref, wide_ref, sems) = refs[3 * count : 5 * count], refs[5 * count :]
    copies = []
    for k, w_ref in enumerate(weights):
        f_ref, b_ref = held[2 * k : 2 * k + 2]
        rows, cols = w_ref.shape
        pitch = b_ref.shape[0] // fields
        line_ref[...] = jnp.zeros(line_ref.shape, F32)
        line_ref[0:rows, 0:cols] = w_ref[...].astype(F32)
        for c in range(0, fields * pitch, 128):
            if c < cols:
                wide_ref[c : c + 128, :] = line_ref[:, c : c + 128].T
            else:
                wide_ref[c : c + 128, :] = jnp.zeros((128, 128), F32)
        for f in range(fields):
            b_ref[f * pitch : (f + 1) * pitch, :] = wide_ref[
                pl.ds(f, pitch, stride=fields), :
            ].astype(BF16)
        copies.append(pltpu.make_async_copy(b_ref, outs[2 * k + 1], sems.at[2 * k + 1]))
        copies[-1].start()
        tall = f_ref.shape[0]
        for c in range(0, fields * pitch, 128):
            width = min(128, fields * pitch - c)
            f_ref[:, c : c + width] = b_ref[c : c + width, :].T[0:tall]
        copies.append(pltpu.make_async_copy(f_ref, outs[2 * k], sems.at[2 * k]))
        copies[-1].start()
    for copy in copies:
        copy.wait()


def call_prep(weights, fields):
    rows = weights[0].shape[0]
    tall = -(-rows // 16) * 16
    shapes = []
    for w in weights:
        pitch = -(-(w.shape[1] // fields) // 16) * 16
        shapes.append(jax.ShapeDtypeStruct((tall, fields * pitch), BF16))
        shapes.append(jax.ShapeDtypeStruct((fields * pitch, 128), BF16))
    deep = max(-(-shape.shape[0] // 128) * 128 for shape in shapes)
    return pl.pallas_call(
        functools.partial(prep_kernel, fields),
        out_shape=tuple(pltpu.HBM(shape.shape, BF16) for shape in shapes),
        in_specs=[VMEM] * len(weights),
        out_specs=tuple([HBM] * len(shapes)),
        scratch_shapes=[pltpu.VMEM(shape.shape, BF16) for shape in shapes]
        + [
            pltpu.VMEM((128, deep), F32),
            pltpu.VMEM((deep, 128), F32),
            pltpu.SemaphoreType.DMA((len(shapes),)),
        ],
        compiler_params=pltpu.CompilerParams(vmem_limit_bytes=14 << 20),
        name="prep",
    )(*weights)


def call_cin(grad_logit, hot_values, hot_line, slot, back, hot_rows, out_weight, forward, backward):
    total, breadth = hot_values.shape
    samples = grad_logit.shape[0]
    lanes = samples * breadth
    owners, slots = back.shape[0], back.shape[0] * back.shape[1]
    tall = forward[0].shape[0]
    small = -(-(FP) // 16) * 16
    fields = backward[0].shape[0] // small
    return pl.pallas_call(
        cin_kernel,
        out_shape=(
            jax.ShapeDtypeStruct((samples,), F32),
            jax.ShapeDtypeStruct((owners, SLOT + hot_rows // owners, breadth), BF16),
        ),
        in_specs=[SMEM] + [VMEM] * 4 + [HBM] * 7,
        out_specs=(SMEM, VMEM),
        scratch_shapes=[
            pltpu.VMEM((total, slots), BF16),
            pltpu.VMEM((128, 128), F32),
            pltpu.VMEM((small, lanes), F32),
            pltpu.VMEM((small, lanes), BF16),
            pltpu.VMEM((tall, lanes), BF16),
            pltpu.VMEM((tall, lanes), BF16),
            pltpu.VMEM((tall, lanes), F32),
            pltpu.VMEM((tall, lanes), F32),
            pltpu.VMEM((fields * tall, lanes), BF16),
            pltpu.VMEM((tall, lanes), F32),
            pltpu.VMEM((FP * 8, lanes), F32),
            pltpu.VMEM((tall, lanes), F32),
            pltpu.VMEM((128, lanes), BF16),
        ]
        + [pltpu.VMEM(x.shape, BF16) for x in (*forward, *backward, hot_values)]
        + [pltpu.SemaphoreType.DMA((7,))],
        compiler_params=pltpu.CompilerParams(vmem_limit_bytes=32 << 20),
        name="cin",
    )(
        grad_logit, hot_line, slot, back.reshape(slots, breadth), out_weight,
        *(
            pltpu.with_memory_space_constraint(x, pltpu.HBM)
            for x in (hot_values, *forward, *backward)
        ),
    )


def merge_kernel(in_ref, ask_ref, out_ref, wide_ref):
    owners = in_ref.shape[0]
    share = in_ref.shape[1] - SLOT
    rows = owners * CAP
    for o in range(owners):
        wide_ref[o * CAP : (o + 1) * CAP, :] = in_ref[o, 0:CAP, :].astype(F32)
    value = wide_ref[...].astype(BF16)
    copies = out_ref.shape[0]
    for c in range(copies):
        out_ref[c, 0:rows, :] = value
    width = 384
    slot = iota((128, width), 1)
    slot = jnp.where(slot < 256, slot, 256 + (slot & 31))
    place = (slot * 7282) >> 16
    rest = slot - place * CAP
    spread = jnp.where(rest == iota((128, width), 0), 1.0, 0.0).astype(BF16)
    keep = place[0:owners] == iota((owners, width), 0)
    ask = jnp.concatenate([ask_ref[...] >> 8, ask_ref[...] & 255], axis=0).astype(F32).astype(BF16)
    wide = jnp.dot(ask, spread, preferred_element_type=F32)
    high = jnp.sum(jnp.where(keep, wide[0:owners], 0.0), axis=0, keepdims=True)
    low = jnp.sum(jnp.where(keep, wide[owners:], 0.0), axis=0, keepdims=True)
    lines = [v[:, n : n + 128] for v in (high, low) for n in range(0, width, 128)]
    lines.append(jnp.zeros((2, 128), F32))
    value = jnp.concatenate(lines, axis=0).astype(BF16)
    for c in range(copies):
        out_ref[c, rows : rows + 8, :] = value
    sums = in_ref[0, SLOT : SLOT + share, :].astype(F32)
    for o in range(1, owners):
        sums = sums + in_ref[o, SLOT : SLOT + share, :].astype(F32)
    value = sums.astype(BF16)
    for c in range(copies):
        out_ref[c, rows + 8 : rows + 8 + share, :] = value


def pack_kernel(rows, *refs):
    blocks, out_ref = refs[:-1], refs[-1]
    height = blocks[0].shape[0]
    last = (len(blocks) - 1) * rows
    sums = jnp.zeros((height - rows, out_ref.shape[1]), F32)
    for c, block in enumerate(blocks):
        at = c * rows if c * rows < last else last + height - rows
        out_ref[at : at + rows, :] = block[0:rows, :]
        sums = sums + block[rows:height, :].astype(F32)
    out_ref[last : last + height - rows, :] = sums.astype(BF16)


def hot_kernel(tops, *refs):
    parts, out_ref = refs[:-1], refs[-1]
    owners, share, breadth = out_ref.shape
    sums = jnp.zeros((share, breadth), F32)
    for part, top in zip(parts, tops):
        if top is not None:
            sums = sums + part[top : top + share, :].astype(F32)
    value = sums.astype(BF16)
    for o in range(owners):
        out_ref[o] = value


def scatter_kernel(places, rows, *refs):
    parts, out_ref, stack_ref, high_ref, low_ref, pick_ref, wide_ref, rhs_ref = refs[:-7], *refs[-7:]
    full = rows // 128 * 128
    tail = rows - full
    per = 128 // tail
    sources = [(parts[n], top) for n, top in places]
    deep = len(sources) * full
    lane = iota((16, 128), 1)
    lines = len(sources) // per
    for n, (part, top) in enumerate(sources):
        stack_ref[n * full : (n + 1) * full, :] = part[top : top + full, :]
        at = deep + n * tail
        stack_ref[at : at + tail, :] = part[top + full : top + rows, :]
    for half, line_ref in ((0, high_ref), (3, low_ref)):
        for n, (part, top) in enumerate(sources):
            ids = part[top + rows : top + rows + 8, :].astype(F32)
            for c in range(full // 128):
                at = n * full + c * 128
                line_ref[:, at : at + 128] = jnp.broadcast_to(
                    ids[half + c : half + c + 1], (16, 128)
                ).astype(BF16)
        for t in range(lines):
            merged = jnp.zeros((16, 128), F32)
            for u in range(per):
                part, top = sources[t * per + u]
                row = part[top + rows : top + rows + 8, :].astype(F32)[half + 2 : half + 3]
                merged = jnp.where(lane // tail == u, jnp.broadcast_to(row, (16, 128)), merged)
            at = deep + t * 128
            line_ref[:, at : at + 128] = merged.astype(BF16)
    depth = stack_ref.shape[0]
    block = pick_ref.shape[0]
    one = jnp.ones((16, 128), BF16)
    zero = jnp.zeros((16, 128), BF16)
    for r in range(0, block, 16):
        place = (iota((16, 128), 0) + r).astype(F32).astype(BF16)
        for n in range(0, depth, 128):
            pick_ref[r : r + 16, n : n + 128] = jnp.where(low_ref[:, n : n + 128] == place, one, zero)
    for n in range(0, depth, 128):
        wide_ref[n : n + 128, :] = (
            jnp.broadcast_to(high_ref[0:1, n : n + 128].astype(F32), (128, 128)).T.astype(BF16)
        )

    def step(t, _):
        for u in range(2):
            for v in range(2):
                mine = jnp.full((16, 128), 4 * t + 2 * u + v, I32).astype(F32).astype(BF16)
                for n in range(0, depth, 16):
                    rhs_ref[u, n : n + 16, v * 128 : (v + 1) * 128] = jnp.where(
                        wide_ref[n : n + 16, :] == mine, stack_ref[n : n + 16, :], zero
                    )
            value = jnp.dot(pick_ref[...], rhs_ref[u], preferred_element_type=F32).astype(BF16)
            for v in range(2):
                at = pl.multiple_of((4 * t + 2 * u + v) * block, block)
                out_ref[pl.ds(at, block), :] = value[:, v * 128 : (v + 1) * 128]
        return 0

    lax.fori_loop(0, out_ref.shape[0] // block // 4, step, 0)


def call_merge(incoming, requested, copies):
    owners, tall, breadth = incoming.shape
    height = owners * CAP + 8 + tall - SLOT
    return pl.pallas_call(
        merge_kernel,
        out_shape=jax.ShapeDtypeStruct((copies, height, breadth), BF16),
        in_specs=[VMEM, VMEM],
        out_specs=VMEM,
        scratch_shapes=[pltpu.VMEM((owners * CAP, breadth), F32)],
        compiler_params=pltpu.CompilerParams(vmem_limit_bytes=4 << 20),
        name="merge",
    )(incoming, requested)


def call_pack(blocks, rows):
    height, breadth = blocks[0].shape
    count = len(blocks)
    return pl.pallas_call(
        functools.partial(pack_kernel, rows),
        out_shape=jax.ShapeDtypeStruct((count * rows + height - rows, breadth), BF16),
        in_specs=[VMEM] * count,
        out_specs=VMEM,
        compiler_params=pltpu.CompilerParams(vmem_limit_bytes=4 << 20),
        name="pack",
    )(*blocks)


def call_hot(parts, tops, owners, share):
    breadth = parts[0].shape[1]
    return pl.pallas_call(
        functools.partial(hot_kernel, tops),
        out_shape=jax.ShapeDtypeStruct((owners, share, breadth), BF16),
        in_specs=[VMEM] * len(parts),
        out_specs=VMEM,
        compiler_params=pltpu.CompilerParams(vmem_limit_bytes=6 << 20),
        name="hot_sum",
    )(*parts)


def call_scatter(parts, places, rows, table_rows):
    breadth = parts[0].shape[1]
    count = len(places)
    block = 256
    return pl.pallas_call(
        functools.partial(scatter_kernel, places, rows),
        out_shape=jax.ShapeDtypeStruct((table_rows, breadth), BF16),
        in_specs=[VMEM] * len(parts),
        out_specs=VMEM,
        scratch_shapes=[
            pltpu.VMEM((count * rows, breadth), BF16),
            pltpu.VMEM((16, count * rows), BF16),
            pltpu.VMEM((16, count * rows), BF16),
            pltpu.VMEM((block, count * rows), BF16),
            pltpu.VMEM((count * rows, breadth), BF16),
            pltpu.VMEM((2, count * rows, 2 * breadth), BF16),
        ],
        compiler_params=pltpu.CompilerParams(vmem_limit_bytes=16 << 20),
        name="cold_scatter",
    )(*parts)


def exchange(block, rows):
    groups = lax.axis_size("group")
    share = block.shape[0] - rows

    def move(x, hop):
        return lax.ppermute(x, "group", [(i, (i + hop) % groups) for i in range(groups)])

    apart = groups // 4
    far = [move(block, apart), move(block, -apart), move(block, 2 * apart)]
    mine = call_pack([far[0], block, far[1], far[2]], rows)
    up, down = move(mine, 1), move(mine, -1)
    up_half = move(up[: 2 * rows], 1)
    down_half = move(down[rows : 3 * rows + share], -1)
    whole = (0, rows, 2 * rows, 3 * rows + share)
    sources = [(n, top) for n in range(3) for top in whole]
    sources += [(n, top) for n in (3, 4) for top in (0, rows)]
    return (mine, up, down, up_half, down_half), sources


def local(
    hot_row, cold_row, cold_owner, is_cold, grad_logit, hot_table, cold_table,
    first_weight, second_weight, third_weight, out_weight,
):
    samples, fields = hot_row.shape
    breadth = hot_table.shape[1]
    owners = lax.axis_size("shard")
    forms = call_prep((first_weight, second_weight, third_weight), fields)
    ask, slot = call_route(cold_row, cold_owner, is_cold, owners)
    hot_values, hot_line = call_hot_rows(hot_row, is_cold, hot_table)
    ask_in = lax.all_to_all(ask, "shard", split_axis=0, concat_axis=0, tiled=True)
    requested = ask_in[:, :SLOT]
    requested, hot_line = lax.optimization_barrier((requested, hot_line))
    found = cold_table.at[requested].get(mode="promise_in_bounds")
    returned = lax.all_to_all(found, "shard", split_axis=0, concat_axis=0, tiled=True)
    logits, outgoing = call_cin(
        grad_logit, hot_values, hot_line, slot, returned, hot_table.shape[0], out_weight,
        forms[0::2], forms[1::2],
    )
    incoming = lax.all_to_all(outgoing, "shard", split_axis=0, concat_axis=0, tiled=True)
    rows = owners * CAP
    share = hot_table.shape[0] // owners
    tall = rows + 8
    block = call_merge(incoming, ask_in, 1)[0]
    parts, places = exchange(block, tall)
    hot_out = lax.all_to_all(
        call_hot(parts, (3 * tall,) * 3 + (None, 2 * tall), owners, share),
        "shard", split_axis=0, concat_axis=0, tiled=True,
    )
    cold_total = call_scatter(parts, places, rows, cold_table.shape[0])
    hot_grad = hot_out.reshape(hot_table.shape)
    return (hot_grad, cold_total, logits)


def solution(mesh):
    across = P(("group", "shard"), None)
    return jax.shard_map(
        local,
        mesh=mesh,
        in_specs=(
            across, across, across, across, P(("group", "shard")), P(), P("shard", None),
            P(), P(), P(), P(),
        ),
        out_specs=(P(), P("shard", None), P(("group", "shard"))),
        check_vma=False,
    )
```

```python
import functools

import jax
import jax.numpy as jnp
from jax import lax
from jax.experimental import pallas as pl
from jax.experimental.pallas import tpu as pltpu
from jax.sharding import PartitionSpec as P

CAP = 9
SLOT = 16
FP = 40
GROUP = 3
VMEM = pl.BlockSpec(memory_space=pltpu.VMEM)
HBM = pl.BlockSpec(memory_space=pltpu.HBM)
SMEM = pl.BlockSpec(memory_space=pltpu.SMEM)
F32 = jnp.float32
BF16 = jnp.bfloat16
I32 = jnp.int32


def iota(shape, dim):
    return lax.broadcasted_iota(I32, shape, dim)


def route_kernel(
    owners, row_hbm, owner_hbm, cold_hbm, ask_ref, slot_ref, want_ref, pad_ref,
    row_ref, owner_ref, cold_ref, sems,
):
    copies = [
        pltpu.make_async_copy(source, target, sems.at[n])
        for n, (source, target) in enumerate(
            ((row_hbm, row_ref), (owner_hbm, owner_ref), (cold_hbm, cold_ref))
        )
    ]
    for copy in copies:
        copy.start()
    for copy in copies:
        copy.wait()
    samples, fields = row_ref.shape
    total = samples * FP
    code = jnp.where(cold_ref[...] == 1, owner_ref[...], -1)
    pad_ref[...] = jnp.full(pad_ref.shape, -1.0, F32)
    pad_ref[0:samples, 0:fields] = code.astype(F32)
    pad_ref[samples : 2 * samples, 0:fields] = row_ref[...].astype(F32)
    turned = pad_ref[...].T
    lane = iota((FP, 128), 1).astype(F32)
    for s in range(samples):
        want_ref[s * FP : (s + 1) * FP, :] = jnp.where(
            turned[0:FP, s : s + 1] == lane, 1.0, 0.0
        )
    wanted = want_ref[...]
    below = (iota((total, total), 0) > iota((total, total), 1)).astype(F32).astype(BF16)
    earlier = jnp.dot(below, wanted.astype(BF16), preferred_element_type=F32)
    position = jnp.sum(earlier * wanted, axis=1, keepdims=True)
    lane_all = iota((total, 128), 1).astype(F32)
    owner_col = jnp.sum(wanted * lane_all, axis=1, keepdims=True)
    is_cold = jnp.sum(wanted, axis=1, keepdims=True)
    slot = jnp.where(is_cold > 0.0, owner_col * SLOT + position, -1.0)
    slot_ref[...] = jnp.broadcast_to(slot, (total, 128)).astype(I32)
    row_col = jnp.concatenate(
        [turned[0:FP, samples + s : samples + s + 1] for s in range(samples)], axis=0
    ).astype(I32)
    at = jnp.broadcast_to(position, (total, 128)) == lane_all
    high = jnp.where(at, (row_col >> 6).astype(F32), 0.0).astype(BF16)
    low = jnp.where(at, (row_col & 63).astype(F32), 0.0).astype(BF16)
    there = jnp.where(at, 1.0, 0.0).astype(BF16)
    turned_want = wanted.T[0:owners, :].astype(BF16)
    asked = jnp.dot(
        turned_want, jnp.concatenate([high, low, there], axis=1), preferred_element_type=F32
    )
    row = asked[:, 0:128] * 64.0 + asked[:, 128:256]
    ask_ref[...] = jnp.where(asked[:, 256:384] > 0.0, row, 0.0).astype(I32)


def cin_kernel(
    gl_ref,
    hot_line_ref,
    slot_ref,
    back_ref,
    scale_ref,
    mix_ref,
    hot_hbm,
    f1_hbm,
    f2_hbm,
    b1_hbm,
    b2_hbm,
    logit_ref,
    outgoing_ref,
    pick_ref,
    out_weight_ref,
    emb_ref,
    embb_ref,
    x2_ref,
    x3_ref,
    w2_ref,
    last_ref,
    outer_ref,
    carry_ref,
    part_ref,
    pool_ref,
    grad_ref,
    f1_ref,
    f2_ref,
    b1_ref,
    b2_ref,
    hot_ref,
    sems,
):
    held = (hot_ref, f1_ref, f2_ref, b2_ref, b1_ref)
    kept = (hot_hbm, f1_hbm, f2_hbm, b2_hbm, b1_hbm)
    copies = [
        pltpu.make_async_copy(source, target, sems.at[n])
        for n, (source, target) in enumerate(zip(kept, held))
    ]
    for copy in copies:
        copy.start()
    samples = gl_ref.shape[0]
    total, breadth = hot_ref.shape
    fields = b1_ref.shape[0] // embb_ref.shape[0]
    lanes = samples * breadth
    slots = back_ref.shape[0]
    owners = outgoing_ref.shape[0]
    share = outgoing_ref.shape[1] - SLOT
    hot_rows = owners * share
    slot = slot_ref[...]
    layers, maps = scale_ref.shape
    tall = carry_ref.shape[0]
    out_weight_ref[...] = jnp.zeros(out_weight_ref.shape, F32)
    out_weight_ref[0:layers, 0:maps] = scale_ref[...]
    out_weight_ref[...] = out_weight_ref[...].T

    for n in range(0, slots, 128):
        pick_ref[:, n : n + 128] = jnp.where(
            slot == iota((total, 128), 1) + n, 1.0, 0.0
        ).astype(BF16)
    copies[0].wait()
    rows = hot_ref[...].astype(F32) + jnp.dot(
        pick_ref[...], back_ref[...], preferred_element_type=F32
    )
    emb_ref[...] = jnp.zeros(emb_ref.shape, F32)
    for s in range(samples):
        emb_ref[0:FP, s * breadth : (s + 1) * breadth] = rows[s * FP : (s + 1) * FP, :]
    embb_ref[...] = emb_ref[...].astype(BF16)

    pool_ref[...] = jnp.zeros(pool_ref.shape, F32)
    states = (embb_ref, x2_ref, x3_ref)
    wides = (emb_ref, w2_ref)
    for k, w_ref in enumerate((f1_ref, f2_ref)):
        source = states[k]
        height = source.shape[0]

        def fill(f, _, source=source, height=height):
            line = jnp.broadcast_to(emb_ref[pl.ds(f, 1), :], (16, lanes)).astype(BF16)
            for r in range(0, height, 16):
                at = pl.multiple_of(f * height + r, 16)
                outer_ref[pl.ds(at, 16), :] = source[r : r + 16, :] * line
            return 0

        lax.fori_loop(0, fields, fill, 0)
        depth = fields * height
        copies[1 + k].wait()
        weight = w_ref[...]
        for n in range(0, lanes, 256):
            value = jnp.dot(
                weight, outer_ref[0:depth, n : n + 256], preferred_element_type=F32
            ).astype(BF16)
            wide = value.astype(F32)
            states[k + 1][:, n : n + 256] = value
            if k < 1:
                wides[k + 1][:, n : n + 256] = wide
            pool_ref[:, n : n + 256] += wide * out_weight_ref[0:tall, k : k + 1]

    mix = mix_ref[...]
    mix_high = mix.astype(BF16)
    mix_low = (mix - mix_high.astype(F32)).astype(BF16)
    small = embb_ref.shape[0]
    turned_high = mix_high.astype(F32).T[0:small, 0:tall].astype(BF16)
    turned_low = mix_low.astype(F32).T[0:small, 0:tall].astype(BF16)
    part_ref[...] = jnp.zeros(part_ref.shape, F32)
    grad_ref[...] = jnp.zeros(grad_ref.shape, BF16)
    for s in range(samples):
        at = slice(s * breadth, (s + 1) * breadth)
        below = jnp.dot(turned_high, x3_ref[:, at], preferred_element_type=F32) + jnp.dot(
            turned_low, x3_ref[:, at], preferred_element_type=F32
        )
        logit_ref[s] = jnp.sum(pool_ref[:, at]) + jnp.sum(below * emb_ref[:, at])
        last_ref[:, at] = below * gl_ref[s]
        across = jnp.dot(
            mix_high[:, 0:small], embb_ref[:, at], preferred_element_type=F32
        ) + jnp.dot(mix_low[:, 0:small], embb_ref[:, at], preferred_element_type=F32)
        carry_ref[:, at] = across * gl_ref[s]

    for k, w_ref in reversed(tuple(enumerate((b1_ref, b2_ref)))):
        copies[4 - k].wait()
        source = wides[k]
        height = source.shape[0]
        for s in range(samples):
            at = slice(s * breadth, (s + 1) * breadth)
            value = jnp.broadcast_to(
                gl_ref[s] * out_weight_ref[0:tall, k : k + 1], (tall, breadth)
            )
            grad_ref[0:tall, at] = (value + carry_ref[:, at]).astype(BF16)
        carry_ref[0:height, :] = jnp.zeros((height, lanes), F32)

        def back(n, _, source=source, height=height, w_ref=w_ref):
            cols = pl.ds(pl.multiple_of(n * 256, 256), 256)
            for t in range(0, fields, GROUP):
                outer = jnp.dot(
                    w_ref[t * height : (t + GROUP) * height, :],
                    grad_ref[:, cols],
                    preferred_element_type=F32,
                )
                sums = [None] * GROUP
                lines = [
                    jnp.broadcast_to(emb_ref[t + u : t + u + 1, cols], (8, 256))
                    for u in range(GROUP)
                ]
                for r in range(0, height, 8):
                    value = source[r : r + 8, cols]
                    total_rows = carry_ref[r : r + 8, cols]
                    for u in range(GROUP):
                        piece = outer[u * height + r : u * height + r + 8]
                        total_rows = total_rows + piece * lines[u]
                        mixed = piece * value
                        sums[u] = mixed if r == 0 else sums[u] + mixed
                    carry_ref[r : r + 8, cols] = total_rows
                for u in range(GROUP):
                    part_ref[(t + u) * 8 : (t + u + 1) * 8, cols] += sums[u]
            return 0

        lax.fori_loop(0, lanes // 256, back, 0)

    grads = carry_ref[0:FP, :] + last_ref[0:FP, :] + jnp.sum(part_ref[...].reshape(FP, 8, lanes), axis=1)
    stacked = jnp.concatenate(
        [grads[:, s * breadth : (s + 1) * breadth] for s in range(samples)], axis=0
    ).astype(BF16)
    slot_line = slot.astype(F32).T[0:1].astype(I32)
    hot_wide = hot_line_ref[0:1]
    line = jnp.where(jnp.broadcast_to(slot_line, (slots, total)) == iota((slots, total), 0), 1.0, 0.0)
    sent_cold = jnp.dot(line.astype(BF16), stacked, preferred_element_type=F32).astype(BF16)
    line = jnp.where(jnp.broadcast_to(hot_wide, (hot_rows, total)) == iota((hot_rows, total), 0), 1.0, 0.0)
    sent_hot = jnp.dot(line.astype(BF16), stacked, preferred_element_type=F32).astype(BF16)
    outgoing_ref[:, 0:SLOT, :] = sent_cold.reshape(owners, SLOT, breadth)
    outgoing_ref[:, SLOT : SLOT + share, :] = sent_hot.reshape(owners, share, breadth)


def call_route(cold_row, cold_owner, is_cold, owners):
    samples, fields = cold_row.shape
    total = samples * FP
    return pl.pallas_call(
        functools.partial(route_kernel, owners),
        out_shape=(
            jax.ShapeDtypeStruct((owners, 128), I32),
            jax.ShapeDtypeStruct((total, 128), I32),
        ),
        in_specs=[HBM] * 3,
        out_specs=(VMEM, VMEM),
        scratch_shapes=[pltpu.VMEM((total, 128), F32), pltpu.VMEM((128, 128), F32)]
        + [pltpu.VMEM((samples, fields), I32)] * 3
        + [pltpu.SemaphoreType.DMA((3,))],
        compiler_params=pltpu.CompilerParams(vmem_limit_bytes=4 << 20),
        name="route",
    )(*(pltpu.with_memory_space_constraint(x, pltpu.HBM) for x in (cold_row, cold_owner, is_cold)))


def hot_rows_kernel(
    hot_ref, cold_ref, table_ref, rows_hbm, line_ref, pad_ref, pick_ref, rows_ref, sem
):
    samples, fields = hot_ref.shape
    total = samples * FP
    hot_rows = table_ref.shape[0]
    pad_ref[...] = jnp.full(pad_ref.shape, -1.0, F32)
    pad_ref[0:samples, 0:fields] = jnp.where(cold_ref[...] == 1, -1, hot_ref[...]).astype(F32)
    turned = pad_ref[...].T
    for s in range(samples):
        ids = turned[0:FP, s : s + 1].astype(I32)
        pick_ref[s * FP : (s + 1) * FP, :] = jnp.where(
            ids == iota((FP, hot_rows), 1), 1.0, 0.0
        ).astype(BF16)
    rows_ref[...] = jnp.dot(
        pick_ref[...], table_ref[...], preferred_element_type=F32
    ).astype(BF16)
    copy = pltpu.make_async_copy(rows_ref, rows_hbm, sem)
    copy.start()
    hot_col = jnp.concatenate([turned[0:FP, s : s + 1] for s in range(samples)], axis=0)
    line_ref[...] = jnp.broadcast_to(hot_col, (total, 128)).T[0:8].astype(I32)
    copy.wait()


def call_hot_rows(hot_row, is_cold, hot_table):
    samples, fields = hot_row.shape
    total = samples * FP
    return pl.pallas_call(
        hot_rows_kernel,
        out_shape=(
            pltpu.HBM((total, hot_table.shape[1]), BF16),
            jax.ShapeDtypeStruct((8, total), I32),
        ),
        in_specs=[VMEM] * 3,
        out_specs=(HBM, VMEM),
        scratch_shapes=[
            pltpu.VMEM((128, 128), F32),
            pltpu.VMEM((total, hot_table.shape[0]), BF16),
            pltpu.VMEM((total, hot_table.shape[1]), BF16),
            pltpu.SemaphoreType.DMA,
        ],
        compiler_params=pltpu.CompilerParams(vmem_limit_bytes=6 << 20),
        name="hot_rows",
    )(hot_row, is_cold, hot_table)


def prep_kernel(fields, *refs):
    count = (len(refs) - 7) // 5
    weights, (third_ref, scale_ref) = refs[0:count], refs[count : count + 2]
    outs, mix_ref = refs[count + 2 : 3 * count + 2], refs[3 * count + 2]
    held = refs[3 * count + 3 : 5 * count + 3]
    line_ref, wide_ref, turn_ref, sems = refs[5 * count + 3 :]
    copies = []
    for k, w_ref in enumerate(weights):
        f_ref, b_ref = held[2 * k : 2 * k + 2]
        rows, cols = w_ref.shape
        pitch = b_ref.shape[0] // fields
        line_ref[...] = jnp.zeros(line_ref.shape, F32)
        line_ref[0:rows, 0:cols] = w_ref[...].astype(F32)
        for c in range(0, fields * pitch, 128):
            if c < cols:
                wide_ref[c : c + 128, :] = line_ref[:, c : c + 128].T
            else:
                wide_ref[c : c + 128, :] = jnp.zeros((128, 128), F32)
        for f in range(fields):
            b_ref[f * pitch : (f + 1) * pitch, :] = wide_ref[
                pl.ds(f, pitch, stride=fields), :
            ].astype(BF16)
        copies.append(pltpu.make_async_copy(b_ref, outs[2 * k + 1], sems.at[2 * k + 1]))
        copies[-1].start()
        tall = f_ref.shape[0]
        for c in range(0, fields * pitch, 128):
            width = min(128, fields * pitch - c)
            f_ref[:, c : c + width] = b_ref[c : c + width, :].T[0:tall]
        copies.append(pltpu.make_async_copy(f_ref, outs[2 * k], sems.at[2 * k]))
        copies[-1].start()
    rows, cols = third_ref.shape
    layers, maps = scale_ref.shape
    turn_ref[...] = jnp.zeros(turn_ref.shape, F32)
    turn_ref[0:layers, 0:maps] = scale_ref[...]
    scale = turn_ref[...].T[:, layers - 1 : layers]
    line_ref[...] = jnp.zeros(line_ref.shape, F32)
    line_ref[0:rows, 0:cols] = third_ref[...].astype(F32)
    tall = mix_ref.shape[0]
    for c in range(0, fields * tall, 128):
        if c < cols:
            total = jnp.sum(line_ref[:, c : c + 128] * scale, axis=0, keepdims=True)
            wide_ref[c : c + 128, :] = jnp.broadcast_to(total, (128, 128)).T
        else:
            wide_ref[c : c + 128, :] = jnp.zeros((128, 128), F32)
    lane = iota((tall, 128), 1)
    mix = jnp.zeros((tall, 128), F32)
    for f in range(fields):
        mix = jnp.where(lane == f, wide_ref[pl.ds(f, tall, stride=fields), :], mix)
    mix_ref[...] = mix
    for copy in copies:
        copy.wait()


def call_prep(weights, third, out_weight, fields):
    rows = weights[0].shape[0]
    tall = -(-rows // 16) * 16
    shapes = []
    for w in weights:
        pitch = -(-(w.shape[1] // fields) // 16) * 16
        shapes.append(jax.ShapeDtypeStruct((tall, fields * pitch), BF16))
        shapes.append(jax.ShapeDtypeStruct((fields * pitch, 128), BF16))
    deep = -(-fields * tall // 128) * 128
    return pl.pallas_call(
        functools.partial(prep_kernel, fields),
        out_shape=tuple(pltpu.HBM(shape.shape, BF16) for shape in shapes)
        + (jax.ShapeDtypeStruct((tall, 128), F32),),
        in_specs=[VMEM] * (len(weights) + 2),
        out_specs=tuple([HBM] * len(shapes)) + (VMEM,),
        scratch_shapes=[pltpu.VMEM(shape.shape, BF16) for shape in shapes]
        + [
            pltpu.VMEM((128, deep), F32),
            pltpu.VMEM((deep, 128), F32),
            pltpu.VMEM((128, 128), F32),
            pltpu.SemaphoreType.DMA((len(shapes),)),
        ],
        compiler_params=pltpu.CompilerParams(vmem_limit_bytes=14 << 20),
        name="prep",
    )(*weights, third, out_weight)


def call_cin(
    grad_logit, hot_values, hot_line, slot, back, hot_rows, out_weight, mix, forward, backward
):
    total, breadth = hot_values.shape
    samples = grad_logit.shape[0]
    lanes = samples * breadth
    owners, slots = back.shape[0], back.shape[0] * back.shape[1]
    tall = forward[0].shape[0]
    small = -(-(FP) // 16) * 16
    fields = backward[0].shape[0] // small
    return pl.pallas_call(
        cin_kernel,
        out_shape=(
            jax.ShapeDtypeStruct((samples,), F32),
            jax.ShapeDtypeStruct((owners, SLOT + hot_rows // owners, breadth), BF16),
        ),
        in_specs=[SMEM] + [VMEM] * 5 + [HBM] * 5,
        out_specs=(SMEM, VMEM),
        scratch_shapes=[
            pltpu.VMEM((total, slots), BF16),
            pltpu.VMEM((128, 128), F32),
            pltpu.VMEM((small, lanes), F32),
            pltpu.VMEM((small, lanes), BF16),
            pltpu.VMEM((tall, lanes), BF16),
            pltpu.VMEM((tall, lanes), BF16),
            pltpu.VMEM((tall, lanes), F32),
            pltpu.VMEM((small, lanes), F32),
            pltpu.VMEM((fields * tall, lanes), BF16),
            pltpu.VMEM((tall, lanes), F32),
            pltpu.VMEM((FP * 8, lanes), F32),
            pltpu.VMEM((tall, lanes), F32),
            pltpu.VMEM((128, lanes), BF16),
        ]
        + [pltpu.VMEM(x.shape, BF16) for x in (*forward, *backward, hot_values)]
        + [pltpu.SemaphoreType.DMA((5,))],
        compiler_params=pltpu.CompilerParams(vmem_limit_bytes=28 << 20),
        name="cin",
    )(
        grad_logit, hot_line, slot, back.reshape(slots, breadth), out_weight, mix,
        *(
            pltpu.with_memory_space_constraint(x, pltpu.HBM)
            for x in (hot_values, *forward, *backward)
        ),
    )


def merge_kernel(in_ref, ask_ref, out_ref, wide_ref):
    owners = in_ref.shape[0]
    share = in_ref.shape[1] - SLOT
    rows = owners * CAP
    for o in range(owners):
        wide_ref[o * CAP : (o + 1) * CAP, :] = in_ref[o, 0:CAP, :].astype(F32)
    value = wide_ref[...].astype(BF16)
    copies = out_ref.shape[0]
    for c in range(copies):
        out_ref[c, 0:rows, :] = value
    width = 384
    slot = iota((128, width), 1)
    slot = jnp.where(slot < 256, slot, 256 + (slot & 31))
    place = (slot * 7282) >> 16
    rest = slot - place * CAP
    spread = jnp.where(rest == iota((128, width), 0), 1.0, 0.0).astype(BF16)
    keep = place[0:owners] == iota((owners, width), 0)
    ask = jnp.concatenate([ask_ref[...] >> 8, ask_ref[...] & 255], axis=0).astype(F32).astype(BF16)
    wide = jnp.dot(ask, spread, preferred_element_type=F32)
    high = jnp.sum(jnp.where(keep, wide[0:owners], 0.0), axis=0, keepdims=True)
    low = jnp.sum(jnp.where(keep, wide[owners:], 0.0), axis=0, keepdims=True)
    lines = [v[:, n : n + 128] for v in (high, low) for n in range(0, width, 128)]
    lines.append(jnp.zeros((2, 128), F32))
    value = jnp.concatenate(lines, axis=0).astype(BF16)
    for c in range(copies):
        out_ref[c, rows : rows + 8, :] = value
    sums = in_ref[0, SLOT : SLOT + share, :].astype(F32)
    for o in range(1, owners):
        sums = sums + in_ref[o, SLOT : SLOT + share, :].astype(F32)
    value = sums.astype(BF16)
    for c in range(copies):
        out_ref[c, rows + 8 : rows + 8 + share, :] = value


def pack_kernel(rows, *refs):
    blocks, out_ref = refs[:-1], refs[-1]
    height = blocks[0].shape[0]
    last = (len(blocks) - 1) * rows
    sums = jnp.zeros((height - rows, out_ref.shape[1]), F32)
    for c, block in enumerate(blocks):
        at = c * rows if c * rows < last else last + height - rows
        out_ref[at : at + rows, :] = block[0:rows, :]
        sums = sums + block[rows:height, :].astype(F32)
    out_ref[last : last + height - rows, :] = sums.astype(BF16)


def hot_kernel(tops, *refs):
    parts, out_ref = refs[:-1], refs[-1]
    owners, share, breadth = out_ref.shape
    sums = jnp.zeros((share, breadth), F32)
    for part, top in zip(parts, tops):
        if top is not None:
            sums = sums + part[top : top + share, :].astype(F32)
    value = sums.astype(BF16)
    for o in range(owners):
        out_ref[o] = value


def scatter_kernel(places, rows, *refs):
    parts, out_ref, stack_ref, high_ref, low_ref, pick_ref, wide_ref, rhs_ref = refs[:-7], *refs[-7:]
    full = rows // 128 * 128
    tail = rows - full
    per = 128 // tail
    sources = [(parts[n], top) for n, top in places]
    deep = len(sources) * full
    lane = iota((16, 128), 1)
    lines = len(sources) // per
    for n, (part, top) in enumerate(sources):
        stack_ref[n * full : (n + 1) * full, :] = part[top : top + full, :]
        at = deep + n * tail
        stack_ref[at : at + tail, :] = part[top + full : top + rows, :]
    for half, line_ref in ((0, high_ref), (3, low_ref)):
        for n, (part, top) in enumerate(sources):
            ids = part[top + rows : top + rows + 8, :].astype(F32)
            for c in range(full // 128):
                at = n * full + c * 128
                line_ref[:, at : at + 128] = jnp.broadcast_to(
                    ids[half + c : half + c + 1], (16, 128)
                ).astype(BF16)
        for t in range(lines):
            merged = jnp.zeros((16, 128), F32)
            for u in range(per):
                part, top = sources[t * per + u]
                row = part[top + rows : top + rows + 8, :].astype(F32)[half + 2 : half + 3]
                merged = jnp.where(lane // tail == u, jnp.broadcast_to(row, (16, 128)), merged)
            at = deep + t * 128
            line_ref[:, at : at + 128] = merged.astype(BF16)
    depth = stack_ref.shape[0]
    block = pick_ref.shape[0]
    one = jnp.ones((16, 128), BF16)
    zero = jnp.zeros((16, 128), BF16)
    for r in range(0, block, 16):
        place = (iota((16, 128), 0) + r).astype(F32).astype(BF16)
        for n in range(0, depth, 128):
            pick_ref[r : r + 16, n : n + 128] = jnp.where(low_ref[:, n : n + 128] == place, one, zero)
    for n in range(0, depth, 128):
        wide_ref[n : n + 128, :] = (
            jnp.broadcast_to(high_ref[0:1, n : n + 128].astype(F32), (128, 128)).T.astype(BF16)
        )

    def step(t, _):
        for u in range(2):
            for v in range(2):
                mine = jnp.full((16, 128), 4 * t + 2 * u + v, I32).astype(F32).astype(BF16)
                for n in range(0, depth, 16):
                    rhs_ref[u, n : n + 16, v * 128 : (v + 1) * 128] = jnp.where(
                        wide_ref[n : n + 16, :] == mine, stack_ref[n : n + 16, :], zero
                    )
            value = jnp.dot(pick_ref[...], rhs_ref[u], preferred_element_type=F32).astype(BF16)
            for v in range(2):
                at = pl.multiple_of((4 * t + 2 * u + v) * block, block)
                out_ref[pl.ds(at, block), :] = value[:, v * 128 : (v + 1) * 128]
        return 0

    lax.fori_loop(0, out_ref.shape[0] // block // 4, step, 0)


def call_merge(incoming, requested, copies):
    owners, tall, breadth = incoming.shape
    height = owners * CAP + 8 + tall - SLOT
    return pl.pallas_call(
        merge_kernel,
        out_shape=jax.ShapeDtypeStruct((copies, height, breadth), BF16),
        in_specs=[VMEM, VMEM],
        out_specs=VMEM,
        scratch_shapes=[pltpu.VMEM((owners * CAP, breadth), F32)],
        compiler_params=pltpu.CompilerParams(vmem_limit_bytes=4 << 20),
        name="merge",
    )(incoming, requested)


def call_pack(blocks, rows):
    height, breadth = blocks[0].shape
    count = len(blocks)
    return pl.pallas_call(
        functools.partial(pack_kernel, rows),
        out_shape=jax.ShapeDtypeStruct((count * rows + height - rows, breadth), BF16),
        in_specs=[VMEM] * count,
        out_specs=VMEM,
        compiler_params=pltpu.CompilerParams(vmem_limit_bytes=4 << 20),
        name="pack",
    )(*blocks)


def call_hot(parts, tops, owners, share):
    breadth = parts[0].shape[1]
    return pl.pallas_call(
        functools.partial(hot_kernel, tops),
        out_shape=jax.ShapeDtypeStruct((owners, share, breadth), BF16),
        in_specs=[VMEM] * len(parts),
        out_specs=VMEM,
        compiler_params=pltpu.CompilerParams(vmem_limit_bytes=6 << 20),
        name="hot_sum",
    )(*parts)


def call_scatter(parts, places, rows, table_rows):
    breadth = parts[0].shape[1]
    count = len(places)
    block = 256
    return pl.pallas_call(
        functools.partial(scatter_kernel, places, rows),
        out_shape=jax.ShapeDtypeStruct((table_rows, breadth), BF16),
        in_specs=[VMEM] * len(parts),
        out_specs=VMEM,
        scratch_shapes=[
            pltpu.VMEM((count * rows, breadth), BF16),
            pltpu.VMEM((16, count * rows), BF16),
            pltpu.VMEM((16, count * rows), BF16),
            pltpu.VMEM((block, count * rows), BF16),
            pltpu.VMEM((count * rows, breadth), BF16),
            pltpu.VMEM((2, count * rows, 2 * breadth), BF16),
        ],
        compiler_params=pltpu.CompilerParams(vmem_limit_bytes=16 << 20),
        name="cold_scatter",
    )(*parts)


def exchange(block, rows):
    groups = lax.axis_size("group")
    share = block.shape[0] - rows

    def move(x, hop):
        return lax.ppermute(x, "group", [(i, (i + hop) % groups) for i in range(groups)])

    apart = groups // 4
    far = [move(block, apart), move(block, -apart), move(block, 2 * apart)]
    mine = call_pack([far[0], block, far[1], far[2]], rows)
    up, down = move(mine, 1), move(mine, -1)
    up_half = move(up[: 2 * rows], 1)
    down_half = move(down[rows : 3 * rows + share], -1)
    whole = (0, rows, 2 * rows, 3 * rows + share)
    sources = [(n, top) for n in range(3) for top in whole]
    sources += [(n, top) for n in (3, 4) for top in (0, rows)]
    return (mine, up, down, up_half, down_half), sources


def local(
    hot_row, cold_row, cold_owner, is_cold, grad_logit, hot_table, cold_table,
    first_weight, second_weight, third_weight, out_weight,
):
    samples, fields = hot_row.shape
    breadth = hot_table.shape[1]
    owners = lax.axis_size("shard")
    *forms, mix = call_prep((first_weight, second_weight), third_weight, out_weight, fields)
    ask, slot = call_route(cold_row, cold_owner, is_cold, owners)
    hot_values, hot_line = call_hot_rows(hot_row, is_cold, hot_table)
    ask_in = lax.all_to_all(ask, "shard", split_axis=0, concat_axis=0, tiled=True)
    requested = ask_in[:, :SLOT]
    requested, hot_line = lax.optimization_barrier((requested, hot_line))
    found = cold_table.at[requested].get(mode="promise_in_bounds")
    returned = lax.all_to_all(found, "shard", split_axis=0, concat_axis=0, tiled=True)
    logits, outgoing = call_cin(
        grad_logit, hot_values, hot_line, slot, returned, hot_table.shape[0], out_weight,
        mix, forms[0::2], forms[1::2],
    )
    incoming = lax.all_to_all(outgoing, "shard", split_axis=0, concat_axis=0, tiled=True)
    rows = owners * CAP
    share = hot_table.shape[0] // owners
    tall = rows + 8
    block = call_merge(incoming, ask_in, 1)[0]
    parts, places = exchange(block, tall)
    hot_out = lax.all_to_all(
        call_hot(parts, (3 * tall,) * 3 + (None, 2 * tall), owners, share),
        "shard", split_axis=0, concat_axis=0, tiled=True,
    )
    cold_total = call_scatter(parts, places, rows, cold_table.shape[0])
    hot_grad = hot_out.reshape(hot_table.shape)
    return (hot_grad, cold_total, logits)


def solution(mesh):
    across = P(("group", "shard"), None)
    return jax.shard_map(
        local,
        mesh=mesh,
        in_specs=(
            across, across, across, across, P(("group", "shard")), P(), P("shard", None),
            P(), P(), P(), P(),
        ),
        out_specs=(P(), P("shard", None), P(("group", "shard"))),
        check_vma=False,
    )
```

```python
import functools

import jax
import jax.numpy as jnp
from jax import lax
from jax.experimental import pallas as pl
from jax.experimental.pallas import tpu as pltpu
from jax.sharding import PartitionSpec as P

CAP = 9
SLOT = 16
FP = 40
GROUP = 3
VMEM = pl.BlockSpec(memory_space=pltpu.VMEM)
HBM = pl.BlockSpec(memory_space=pltpu.HBM)
SMEM = pl.BlockSpec(memory_space=pltpu.SMEM)
F32 = jnp.float32
BF16 = jnp.bfloat16
I32 = jnp.int32


def iota(shape, dim):
    return lax.broadcasted_iota(I32, shape, dim)


def route_kernel(
    owners, row_hbm, owner_hbm, cold_hbm, ask_ref, slot_ref, want_ref, pad_ref,
    row_ref, owner_ref, cold_ref, sems,
):
    copies = [
        pltpu.make_async_copy(source, target, sems.at[n])
        for n, (source, target) in enumerate(
            ((row_hbm, row_ref), (owner_hbm, owner_ref), (cold_hbm, cold_ref))
        )
    ]
    for copy in copies:
        copy.start()
    for copy in copies:
        copy.wait()
    samples, fields = row_ref.shape
    total = samples * FP
    code = jnp.where(cold_ref[...] == 1, owner_ref[...], -1)
    pad_ref[...] = jnp.full(pad_ref.shape, -1.0, F32)
    pad_ref[0:samples, 0:fields] = code.astype(F32)
    pad_ref[samples : 2 * samples, 0:fields] = row_ref[...].astype(F32)
    turned = pad_ref[...].T
    lane = iota((FP, 128), 1).astype(F32)
    for s in range(samples):
        want_ref[s * FP : (s + 1) * FP, :] = jnp.where(
            turned[0:FP, s : s + 1] == lane, 1.0, 0.0
        )
    wanted = want_ref[...]
    below = (iota((total, total), 0) > iota((total, total), 1)).astype(F32).astype(BF16)
    earlier = jnp.dot(below, wanted.astype(BF16), preferred_element_type=F32)
    position = jnp.sum(earlier * wanted, axis=1, keepdims=True)
    lane_all = iota((total, 128), 1).astype(F32)
    owner_col = jnp.sum(wanted * lane_all, axis=1, keepdims=True)
    is_cold = jnp.sum(wanted, axis=1, keepdims=True)
    slot = jnp.where(is_cold > 0.0, owner_col * SLOT + position, -1.0)
    slot_ref[...] = jnp.broadcast_to(slot, (total, 128)).astype(I32)
    row_col = jnp.concatenate(
        [turned[0:FP, samples + s : samples + s + 1] for s in range(samples)], axis=0
    ).astype(I32)
    at = jnp.broadcast_to(position, (total, 128)) == lane_all
    high = jnp.where(at, (row_col >> 6).astype(F32), 0.0).astype(BF16)
    low = jnp.where(at, (row_col & 63).astype(F32), 0.0).astype(BF16)
    there = jnp.where(at, 1.0, 0.0).astype(BF16)
    turned_want = wanted.T[0:owners, :].astype(BF16)
    asked = jnp.dot(
        turned_want, jnp.concatenate([high, low, there], axis=1), preferred_element_type=F32
    )
    row = asked[:, 0:128] * 64.0 + asked[:, 128:256]
    ask_ref[...] = jnp.where(asked[:, 256:384] > 0.0, row, 0.0).astype(I32)


def cin_kernel(
    gl_ref,
    hot_line_ref,
    slot_ref,
    back_ref,
    scale_ref,
    mix_ref,
    hot_hbm,
    f1_hbm,
    f2_hbm,
    b1_hbm,
    b2_hbm,
    logit_ref,
    outgoing_ref,
    pick_ref,
    out_weight_ref,
    emb_ref,
    embb_ref,
    x2_ref,
    x3_ref,
    w2_ref,
    last_ref,
    outer_ref,
    carry_ref,
    part_ref,
    pool_ref,
    grad_ref,
    f1_ref,
    f2_ref,
    b1_ref,
    b2_ref,
    hot_ref,
    sems,
):
    held = (hot_ref, f1_ref, f2_ref, b2_ref, b1_ref)
    kept = (hot_hbm, f1_hbm, f2_hbm, b2_hbm, b1_hbm)
    copies = [
        pltpu.make_async_copy(source, target, sems.at[n])
        for n, (source, target) in enumerate(zip(kept, held))
    ]
    for copy in copies:
        copy.start()
    samples = gl_ref.shape[0]
    total, breadth = hot_ref.shape
    fields = b1_ref.shape[0] // embb_ref.shape[0]
    lanes = samples * breadth
    slots = back_ref.shape[0]
    owners = outgoing_ref.shape[0]
    share = outgoing_ref.shape[1] - SLOT
    hot_rows = owners * share
    slot = slot_ref[...]
    layers, maps = scale_ref.shape
    tall = carry_ref.shape[0]
    out_weight_ref[...] = jnp.zeros(out_weight_ref.shape, F32)
    out_weight_ref[0:layers, 0:maps] = scale_ref[...]
    out_weight_ref[...] = out_weight_ref[...].T

    for n in range(0, slots, 128):
        pick_ref[:, n : n + 128] = jnp.where(
            slot == iota((total, 128), 1) + n, 1.0, 0.0
        ).astype(BF16)
    copies[0].wait()
    rows = hot_ref[...].astype(F32) + jnp.dot(
        pick_ref[...], back_ref[...], preferred_element_type=F32
    )
    emb_ref[...] = jnp.zeros(emb_ref.shape, F32)
    for s in range(samples):
        emb_ref[0:FP, s * breadth : (s + 1) * breadth] = rows[s * FP : (s + 1) * FP, :]
    embb_ref[...] = emb_ref[...].astype(BF16)

    pool_ref[...] = jnp.zeros(pool_ref.shape, F32)
    states = (embb_ref, x2_ref, x3_ref)
    wides = (emb_ref, w2_ref)
    for k, w_ref in enumerate((f1_ref, f2_ref)):
        source = states[k]
        height = source.shape[0]

        def fill(f, _, source=source, height=height):
            line = jnp.broadcast_to(emb_ref[pl.ds(f, 1), :], (16, lanes)).astype(BF16)
            for r in range(0, height, 16):
                at = pl.multiple_of(f * height + r, 16)
                outer_ref[pl.ds(at, 16), :] = source[r : r + 16, :] * line
            return 0

        lax.fori_loop(0, fields, fill, 0)
        depth = fields * height
        copies[1 + k].wait()
        weight = w_ref[...]
        for n in range(0, lanes, 256):
            value = jnp.dot(
                weight, outer_ref[0:depth, n : n + 256], preferred_element_type=F32
            ).astype(BF16)
            wide = value.astype(F32)
            states[k + 1][:, n : n + 256] = value
            if k < 1:
                wides[k + 1][:, n : n + 256] = wide
            pool_ref[:, n : n + 256] += wide * out_weight_ref[0:tall, k : k + 1]

    mix = mix_ref[...]
    mix_high = mix.astype(BF16)
    mix_low = (mix - mix_high.astype(F32)).astype(BF16)
    small = embb_ref.shape[0]
    turned_high = mix_high.astype(F32).T[0:small, 0:tall].astype(BF16)
    turned_low = mix_low.astype(F32).T[0:small, 0:tall].astype(BF16)
    part_ref[...] = jnp.zeros(part_ref.shape, F32)
    grad_ref[...] = jnp.zeros(grad_ref.shape, BF16)
    for s in range(samples):
        at = slice(s * breadth, (s + 1) * breadth)
        below = jnp.dot(turned_high, x3_ref[:, at], preferred_element_type=F32) + jnp.dot(
            turned_low, x3_ref[:, at], preferred_element_type=F32
        )
        logit_ref[s] = jnp.sum(pool_ref[:, at]) + jnp.sum(below * emb_ref[:, at])
        last_ref[:, at] = below * gl_ref[s]
        across = jnp.dot(
            mix_high[:, 0:small], embb_ref[:, at], preferred_element_type=F32
        ) + jnp.dot(mix_low[:, 0:small], embb_ref[:, at], preferred_element_type=F32)
        carry_ref[:, at] = across * gl_ref[s]

    for k, w_ref in reversed(tuple(enumerate((b1_ref, b2_ref)))):
        copies[4 - k].wait()
        source = wides[k]
        height = source.shape[0]
        for s in range(samples):
            at = slice(s * breadth, (s + 1) * breadth)
            value = jnp.broadcast_to(
                gl_ref[s] * out_weight_ref[0:tall, k : k + 1], (tall, breadth)
            )
            grad_ref[0:tall, at] = (value + carry_ref[:, at]).astype(BF16)
        carry_ref[0:height, :] = jnp.zeros((height, lanes), F32)

        def back(n, _, source=source, height=height, w_ref=w_ref):
            cols = pl.ds(pl.multiple_of(n * 256, 256), 256)
            for t in range(0, fields, GROUP):
                outer = jnp.dot(
                    w_ref[t * height : (t + GROUP) * height, :],
                    grad_ref[:, cols],
                    preferred_element_type=F32,
                )
                sums = [None] * GROUP
                lines = [
                    jnp.broadcast_to(emb_ref[t + u : t + u + 1, cols], (8, 256))
                    for u in range(GROUP)
                ]
                for r in range(0, height, 8):
                    value = source[r : r + 8, cols]
                    total_rows = carry_ref[r : r + 8, cols]
                    for u in range(GROUP):
                        piece = outer[u * height + r : u * height + r + 8]
                        total_rows = total_rows + piece * lines[u]
                        mixed = piece * value
                        sums[u] = mixed if r == 0 else sums[u] + mixed
                    carry_ref[r : r + 8, cols] = total_rows
                for u in range(GROUP):
                    part_ref[(t + u) * 8 : (t + u + 1) * 8, cols] += sums[u]
            return 0

        lax.fori_loop(0, lanes // 256, back, 0)

    grads = carry_ref[0:FP, :] + last_ref[0:FP, :] + jnp.sum(part_ref[...].reshape(FP, 8, lanes), axis=1)
    stacked = jnp.concatenate(
        [grads[:, s * breadth : (s + 1) * breadth] for s in range(samples)], axis=0
    ).astype(BF16)
    slot_line = slot.astype(F32).T[0:1].astype(I32)
    hot_wide = hot_line_ref[0:1]
    line = jnp.where(jnp.broadcast_to(slot_line, (slots, total)) == iota((slots, total), 0), 1.0, 0.0)
    sent_cold = jnp.dot(line.astype(BF16), stacked, preferred_element_type=F32).astype(BF16)
    line = jnp.where(jnp.broadcast_to(hot_wide, (hot_rows, total)) == iota((hot_rows, total), 0), 1.0, 0.0)
    sent_hot = jnp.dot(line.astype(BF16), stacked, preferred_element_type=F32).astype(BF16)
    outgoing_ref[:, 0:SLOT, :] = sent_cold.reshape(owners, SLOT, breadth)
    outgoing_ref[:, SLOT : SLOT + share, :] = sent_hot.reshape(owners, share, breadth)


def call_route(cold_row, cold_owner, is_cold, owners):
    samples, fields = cold_row.shape
    total = samples * FP
    return pl.pallas_call(
        functools.partial(route_kernel, owners),
        out_shape=(
            jax.ShapeDtypeStruct((owners, 128), I32),
            jax.ShapeDtypeStruct((total, 128), I32),
        ),
        in_specs=[HBM] * 3,
        out_specs=(VMEM, VMEM),
        scratch_shapes=[pltpu.VMEM((total, 128), F32), pltpu.VMEM((128, 128), F32)]
        + [pltpu.VMEM((samples, fields), I32)] * 3
        + [pltpu.SemaphoreType.DMA((3,))],
        compiler_params=pltpu.CompilerParams(vmem_limit_bytes=4 << 20),
        name="route",
    )(*(pltpu.with_memory_space_constraint(x, pltpu.HBM) for x in (cold_row, cold_owner, is_cold)))


def hot_rows_kernel(
    hot_ref, cold_ref, table_ref, rows_hbm, line_ref, pad_ref, pick_ref, rows_ref, sem
):
    samples, fields = hot_ref.shape
    total = samples * FP
    hot_rows = table_ref.shape[0]
    pad_ref[...] = jnp.full(pad_ref.shape, -1.0, F32)
    pad_ref[0:samples, 0:fields] = jnp.where(cold_ref[...] == 1, -1, hot_ref[...]).astype(F32)
    turned = pad_ref[...].T
    for s in range(samples):
        ids = turned[0:FP, s : s + 1].astype(I32)
        pick_ref[s * FP : (s + 1) * FP, :] = jnp.where(
            ids == iota((FP, hot_rows), 1), 1.0, 0.0
        ).astype(BF16)
    rows_ref[...] = jnp.dot(
        pick_ref[...], table_ref[...], preferred_element_type=F32
    ).astype(BF16)
    copy = pltpu.make_async_copy(rows_ref, rows_hbm, sem)
    copy.start()
    hot_col = jnp.concatenate([turned[0:FP, s : s + 1] for s in range(samples)], axis=0)
    line_ref[...] = jnp.broadcast_to(hot_col, (total, 128)).T[0:8].astype(I32)
    copy.wait()


def call_hot_rows(hot_row, is_cold, hot_table):
    samples, _ = hot_row.shape
    total = samples * FP
    return pl.pallas_call(
        hot_rows_kernel,
        out_shape=(
            pltpu.HBM((total, hot_table.shape[1]), BF16),
            jax.ShapeDtypeStruct((8, total), I32),
        ),
        in_specs=[VMEM] * 3,
        out_specs=(HBM, VMEM),
        scratch_shapes=[
            pltpu.VMEM((128, 128), F32),
            pltpu.VMEM((total, hot_table.shape[0]), BF16),
            pltpu.VMEM((total, hot_table.shape[1]), BF16),
            pltpu.SemaphoreType.DMA,
        ],
        compiler_params=pltpu.CompilerParams(vmem_limit_bytes=6 << 20),
        name="hot_rows",
    )(hot_row, is_cold, hot_table)


def prep_kernel(fields, *refs):
    count = (len(refs) - 7) // 5
    weights, (third_ref, scale_ref) = refs[0:count], refs[count : count + 2]
    outs, mix_ref = refs[count + 2 : 3 * count + 2], refs[3 * count + 2]
    held = refs[3 * count + 3 : 5 * count + 3]
    line_ref, wide_ref, turn_ref, sems = refs[5 * count + 3 :]
    copies = []
    for k, w_ref in enumerate(weights):
        f_ref, b_ref = held[2 * k : 2 * k + 2]
        rows, cols = w_ref.shape
        pitch = b_ref.shape[0] // fields
        line_ref[...] = jnp.zeros(line_ref.shape, F32)
        line_ref[0:rows, 0:cols] = w_ref[...].astype(F32)
        for c in range(0, fields * pitch, 128):
            if c < cols:
                wide_ref[c : c + 128, :] = line_ref[:, c : c + 128].T
            else:
                wide_ref[c : c + 128, :] = jnp.zeros((128, 128), F32)
        for f in range(fields):
            b_ref[f * pitch : (f + 1) * pitch, :] = wide_ref[
                pl.ds(f, pitch, stride=fields), :
            ].astype(BF16)
        copies.append(pltpu.make_async_copy(b_ref, outs[2 * k + 1], sems.at[2 * k + 1]))
        copies[-1].start()
        tall = f_ref.shape[0]
        for c in range(0, fields * pitch, 128):
            width = min(128, fields * pitch - c)
            f_ref[:, c : c + width] = b_ref[c : c + width, :].T[0:tall]
        copies.append(pltpu.make_async_copy(f_ref, outs[2 * k], sems.at[2 * k]))
        copies[-1].start()
    rows, cols = third_ref.shape
    layers, maps = scale_ref.shape
    turn_ref[...] = jnp.zeros(turn_ref.shape, F32)
    turn_ref[0:layers, 0:maps] = scale_ref[...]
    scale = turn_ref[...].T[:, layers - 1 : layers]
    line_ref[...] = jnp.zeros(line_ref.shape, F32)
    line_ref[0:rows, 0:cols] = third_ref[...].astype(F32)
    tall = mix_ref.shape[0]
    for c in range(0, fields * tall, 128):
        if c < cols:
            total = jnp.sum(line_ref[:, c : c + 128] * scale, axis=0, keepdims=True)
            wide_ref[c : c + 128, :] = jnp.broadcast_to(total, (128, 128)).T
        else:
            wide_ref[c : c + 128, :] = jnp.zeros((128, 128), F32)
    lane = iota((tall, 128), 1)
    mix = jnp.zeros((tall, 128), F32)
    for f in range(fields):
        mix = jnp.where(lane == f, wide_ref[pl.ds(f, tall, stride=fields), :], mix)
    mix_ref[...] = mix
    for copy in copies:
        copy.wait()


def call_prep(weights, third, out_weight, fields):
    rows = weights[0].shape[0]
    tall = -(-rows // 16) * 16
    shapes = []
    for w in weights:
        pitch = -(-(w.shape[1] // fields) // 16) * 16
        shapes.append(jax.ShapeDtypeStruct((tall, fields * pitch), BF16))
        shapes.append(jax.ShapeDtypeStruct((fields * pitch, 128), BF16))
    deep = -(-fields * tall // 128) * 128
    return pl.pallas_call(
        functools.partial(prep_kernel, fields),
        out_shape=tuple(pltpu.HBM(shape.shape, BF16) for shape in shapes)
        + (jax.ShapeDtypeStruct((tall, 128), F32),),
        in_specs=[VMEM] * (len(weights) + 2),
        out_specs=tuple([HBM] * len(shapes)) + (VMEM,),
        scratch_shapes=[pltpu.VMEM(shape.shape, BF16) for shape in shapes]
        + [
            pltpu.VMEM((128, deep), F32),
            pltpu.VMEM((deep, 128), F32),
            pltpu.VMEM((128, 128), F32),
            pltpu.SemaphoreType.DMA((len(shapes),)),
        ],
        compiler_params=pltpu.CompilerParams(vmem_limit_bytes=14 << 20),
        name="prep",
    )(*weights, third, out_weight)


def call_cin(
    grad_logit, hot_values, hot_line, slot, back, hot_rows, out_weight, mix, forward, backward
):
    total, breadth = hot_values.shape
    samples = grad_logit.shape[0]
    lanes = samples * breadth
    owners, slots = back.shape[0], back.shape[0] * back.shape[1]
    tall = forward[0].shape[0]
    small = -(-(FP) // 16) * 16
    fields = backward[0].shape[0] // small
    return pl.pallas_call(
        cin_kernel,
        out_shape=(
            jax.ShapeDtypeStruct((samples,), F32),
            jax.ShapeDtypeStruct((owners, SLOT + hot_rows // owners, breadth), BF16),
        ),
        in_specs=[SMEM] + [VMEM] * 5 + [HBM] * 5,
        out_specs=(SMEM, VMEM),
        scratch_shapes=[
            pltpu.VMEM((total, slots), BF16),
            pltpu.VMEM((128, 128), F32),
            pltpu.VMEM((small, lanes), F32),
            pltpu.VMEM((small, lanes), BF16),
            pltpu.VMEM((tall, lanes), BF16),
            pltpu.VMEM((tall, lanes), BF16),
            pltpu.VMEM((tall, lanes), F32),
            pltpu.VMEM((small, lanes), F32),
            pltpu.VMEM((fields * tall, lanes), BF16),
            pltpu.VMEM((tall, lanes), F32),
            pltpu.VMEM((FP * 8, lanes), F32),
            pltpu.VMEM((tall, lanes), F32),
            pltpu.VMEM((128, lanes), BF16),
        ]
        + [pltpu.VMEM(x.shape, BF16) for x in (*forward, *backward, hot_values)]
        + [pltpu.SemaphoreType.DMA((5,))],
        compiler_params=pltpu.CompilerParams(vmem_limit_bytes=28 << 20),
        name="cin",
    )(
        grad_logit, hot_line, slot, back.reshape(slots, breadth), out_weight, mix,
        *(
            pltpu.with_memory_space_constraint(x, pltpu.HBM)
            for x in (hot_values, *forward, *backward)
        ),
    )


def merge_kernel(in_ref, ask_ref, out_ref, wide_ref):
    owners = in_ref.shape[0]
    share = in_ref.shape[1] - SLOT
    rows = owners * CAP
    for o in range(owners):
        wide_ref[o * CAP : (o + 1) * CAP, :] = in_ref[o, 0:CAP, :].astype(F32)
    value = wide_ref[...].astype(BF16)
    copies = out_ref.shape[0]
    for c in range(copies):
        out_ref[c, 0:rows, :] = value
    width = 384
    slot = iota((128, width), 1)
    slot = jnp.where(slot < 256, slot, 256 + (slot & 31))
    place = (slot * 7282) >> 16
    rest = slot - place * CAP
    spread = jnp.where(rest == iota((128, width), 0), 1.0, 0.0).astype(BF16)
    keep = place[0:owners] == iota((owners, width), 0)
    ask = jnp.concatenate([ask_ref[...] >> 8, ask_ref[...] & 255], axis=0).astype(F32).astype(BF16)
    wide = jnp.dot(ask, spread, preferred_element_type=F32)
    high = jnp.sum(jnp.where(keep, wide[0:owners], 0.0), axis=0, keepdims=True)
    low = jnp.sum(jnp.where(keep, wide[owners:], 0.0), axis=0, keepdims=True)
    lines = [v[:, n : n + 128] for v in (high, low) for n in range(0, width, 128)]
    lines.append(jnp.zeros((2, 128), F32))
    value = jnp.concatenate(lines, axis=0).astype(BF16)
    for c in range(copies):
        out_ref[c, rows : rows + 8, :] = value
    sums = in_ref[0, SLOT : SLOT + share, :].astype(F32)
    for o in range(1, owners):
        sums = sums + in_ref[o, SLOT : SLOT + share, :].astype(F32)
    value = sums.astype(BF16)
    for c in range(copies):
        out_ref[c, rows + 8 : rows + 8 + share, :] = value


def pack_kernel(rows, *refs):
    blocks, out_ref = refs[:-1], refs[-1]
    height = blocks[0].shape[0]
    last = (len(blocks) - 1) * rows
    sums = jnp.zeros((height - rows, out_ref.shape[1]), F32)
    for c, block in enumerate(blocks):
        at = c * rows if c * rows < last else last + height - rows
        out_ref[at : at + rows, :] = block[0:rows, :]
        sums = sums + block[rows:height, :].astype(F32)
    out_ref[last : last + height - rows, :] = sums.astype(BF16)


def hot_kernel(tops, *refs):
    parts, out_ref = refs[:-1], refs[-1]
    owners, share, breadth = out_ref.shape
    sums = jnp.zeros((share, breadth), F32)
    for part, top in zip(parts, tops):
        if top is not None:
            sums = sums + part[top : top + share, :].astype(F32)
    value = sums.astype(BF16)
    for o in range(owners):
        out_ref[o] = value


def scatter_kernel(places, rows, *refs):
    parts, out_ref, stack_ref, high_ref, low_ref, pick_ref, wide_ref, rhs_ref = refs[:-7], *refs[-7:]
    full = rows // 128 * 128
    tail = rows - full
    per = 128 // tail
    sources = [(parts[n], top) for n, top in places]
    deep = len(sources) * full
    lane = iota((16, 128), 1)
    lines = len(sources) // per
    for n, (part, top) in enumerate(sources):
        stack_ref[n * full : (n + 1) * full, :] = part[top : top + full, :]
        at = deep + n * tail
        stack_ref[at : at + tail, :] = part[top + full : top + rows, :]
    for half, line_ref in ((0, high_ref), (3, low_ref)):
        for n, (part, top) in enumerate(sources):
            ids = part[top + rows : top + rows + 8, :].astype(F32)
            for c in range(full // 128):
                at = n * full + c * 128
                line_ref[:, at : at + 128] = jnp.broadcast_to(
                    ids[half + c : half + c + 1], (16, 128)
                ).astype(BF16)
        for t in range(lines):
            merged = jnp.zeros((16, 128), F32)
            for u in range(per):
                part, top = sources[t * per + u]
                row = part[top + rows : top + rows + 8, :].astype(F32)[half + 2 : half + 3]
                merged = jnp.where(lane // tail == u, jnp.broadcast_to(row, (16, 128)), merged)
            at = deep + t * 128
            line_ref[:, at : at + 128] = merged.astype(BF16)
    depth = stack_ref.shape[0]
    block = pick_ref.shape[0]
    one = jnp.ones((16, 128), BF16)
    zero = jnp.zeros((16, 128), BF16)
    for r in range(0, block, 16):
        place = (iota((16, 128), 0) + r).astype(F32).astype(BF16)
        for n in range(0, depth, 128):
            pick_ref[r : r + 16, n : n + 128] = jnp.where(low_ref[:, n : n + 128] == place, one, zero)
    for n in range(0, depth, 128):
        wide_ref[n : n + 128, :] = (
            jnp.broadcast_to(high_ref[0:1, n : n + 128].astype(F32), (128, 128)).T.astype(BF16)
        )

    def step(t, _):
        for u in range(2):
            for v in range(2):
                mine = jnp.full((16, 128), 4 * t + 2 * u + v, I32).astype(F32).astype(BF16)
                for n in range(0, depth, 16):
                    rhs_ref[u, n : n + 16, v * 128 : (v + 1) * 128] = jnp.where(
                        wide_ref[n : n + 16, :] == mine, stack_ref[n : n + 16, :], zero
                    )
            value = jnp.dot(pick_ref[...], rhs_ref[u], preferred_element_type=F32).astype(BF16)
            for v in range(2):
                at = pl.multiple_of((4 * t + 2 * u + v) * block, block)
                out_ref[pl.ds(at, block), :] = value[:, v * 128 : (v + 1) * 128]
        return 0

    lax.fori_loop(0, out_ref.shape[0] // block // 4, step, 0)


def call_merge(incoming, requested, copies):
    owners, tall, breadth = incoming.shape
    height = owners * CAP + 8 + tall - SLOT
    return pl.pallas_call(
        merge_kernel,
        out_shape=jax.ShapeDtypeStruct((copies, height, breadth), BF16),
        in_specs=[VMEM, VMEM],
        out_specs=VMEM,
        scratch_shapes=[pltpu.VMEM((owners * CAP, breadth), F32)],
        compiler_params=pltpu.CompilerParams(vmem_limit_bytes=4 << 20),
        name="merge",
    )(incoming, requested)


def call_pack(blocks, rows):
    height, breadth = blocks[0].shape
    count = len(blocks)
    return pl.pallas_call(
        functools.partial(pack_kernel, rows),
        out_shape=jax.ShapeDtypeStruct((count * rows + height - rows, breadth), BF16),
        in_specs=[VMEM] * count,
        out_specs=VMEM,
        compiler_params=pltpu.CompilerParams(vmem_limit_bytes=4 << 20),
        name="pack",
    )(*blocks)


def call_hot(parts, tops, owners, share):
    breadth = parts[0].shape[1]
    return pl.pallas_call(
        functools.partial(hot_kernel, tops),
        out_shape=jax.ShapeDtypeStruct((owners, share, breadth), BF16),
        in_specs=[VMEM] * len(parts),
        out_specs=VMEM,
        compiler_params=pltpu.CompilerParams(vmem_limit_bytes=6 << 20),
        name="hot_sum",
    )(*parts)


def call_scatter(parts, places, rows, table_rows):
    breadth = parts[0].shape[1]
    count = len(places)
    block = 256
    return pl.pallas_call(
        functools.partial(scatter_kernel, places, rows),
        out_shape=jax.ShapeDtypeStruct((table_rows, breadth), BF16),
        in_specs=[VMEM] * len(parts),
        out_specs=VMEM,
        scratch_shapes=[
            pltpu.VMEM((count * rows, breadth), BF16),
            pltpu.VMEM((16, count * rows), BF16),
            pltpu.VMEM((16, count * rows), BF16),
            pltpu.VMEM((block, count * rows), BF16),
            pltpu.VMEM((count * rows, breadth), BF16),
            pltpu.VMEM((2, count * rows, 2 * breadth), BF16),
        ],
        compiler_params=pltpu.CompilerParams(vmem_limit_bytes=16 << 20),
        name="cold_scatter",
    )(*parts)


def exchange(block, rows):
    groups = lax.axis_size("group")
    share = block.shape[0] - rows

    def move(x, hop):
        return lax.ppermute(x, "group", [(i, (i + hop) % groups) for i in range(groups)])

    apart = groups // 4
    far = [move(block, apart), move(block, -apart), move(block, 2 * apart)]
    mine = call_pack([far[0], block, far[1], far[2]], rows)
    up, down = move(mine, 1), move(mine, -1)
    up_tail = up[: 2 * rows]
    up_half = move(up_tail, 1)
    down_half = move(down[rows : 3 * rows + share], -1)
    whole = (0, rows, 2 * rows, 3 * rows + share)
    sources = [(n, top) for n in range(3) for top in whole]
    sources += [(n, top) for n in (3, 4) for top in (0, rows)]
    return (mine, up, down, up_half, down_half), sources


def local(
    hot_row, cold_row, cold_owner, is_cold, grad_logit, hot_table, cold_table,
    first_weight, second_weight, third_weight, out_weight,
):
    _, fields = hot_row.shape
    owners = lax.axis_size("shard")
    *forms, mix = call_prep((first_weight, second_weight), third_weight, out_weight, fields)
    ask, slot = call_route(cold_row, cold_owner, is_cold, owners)
    hot_values, hot_line = call_hot_rows(hot_row, is_cold, hot_table)
    ask_in = lax.all_to_all(ask, "shard", split_axis=0, concat_axis=0, tiled=True)
    requested = ask_in[:, :SLOT]
    requested, hot_line = lax.optimization_barrier((requested, hot_line))
    found = cold_table.at[requested].get(mode="promise_in_bounds")
    returned = lax.all_to_all(found, "shard", split_axis=0, concat_axis=0, tiled=True)
    logits, outgoing = call_cin(
        grad_logit, hot_values, hot_line, slot, returned, hot_table.shape[0], out_weight,
        mix, forms[0::2], forms[1::2],
    )
    incoming = lax.all_to_all(outgoing, "shard", split_axis=0, concat_axis=0, tiled=True)
    rows = owners * CAP
    share = hot_table.shape[0] // owners
    tall = rows + 8
    block = call_merge(incoming, ask_in, 1)[0]
    parts, places = exchange(block, tall)
    hot_part = call_hot(
        (*parts[0:3], parts[4]), (3 * tall,) * 3 + (2 * tall,), owners, share
    )
    hot_out = lax.all_to_all(hot_part, "shard", split_axis=0, concat_axis=0, tiled=True)
    cold_total = call_scatter(parts, places, rows, cold_table.shape[0])
    hot_grad = hot_out.reshape(hot_table.shape)
    return (hot_grad, cold_total, logits)


def solution(mesh):
    across = P(("group", "shard"), None)
    return jax.shard_map(
        local,
        mesh=mesh,
        in_specs=(
            across, across, across, across, P(("group", "shard")), P(), P("shard", None),
            P(), P(), P(), P(),
        ),
        out_specs=(P(), P("shard", None), P(("group", "shard"))),
        check_vma=False,
    )
```
